128 devices in a mesh: sector: 8 (over x_hi, z), group: 16 (over y, x_lo, core).
Axes of the slice: x: 4 (x_hi: 2, x_lo: 2; x = x_hi * 2 + x_lo), y: 4, z: 4, core: 2. Of those that a mesh axis runs over, the one named last changes fastest.
Arguments:
- spectrum: float32 [1152, 128, 1024], P('group', None, 'sector'), may hold values from 0.1 to 2
- land_mask: int32 [128, 1024], P(None, 'sector'), may hold values 0 or 1
- wind_field: float32 [2, 128, 1024], P(None, 'group', 'sector'), may hold values from -3 to 3
- assignment: int32 [1152], replicated, may hold values from 0 to 1151, each once
- courant: float32 [32], replicated, may hold values from 0.3 to 0.65
- growth: float32 [32], replicated, may hold values from 0.1 to 0.5
- whitecap: float32 [32], replicated, may hold values from 0.2 to 1
- weights: float32 [32], replicated, may hold values from 0.5 to 5
- spread: float32 [32, 36, 36], replicated, may hold values from -1 to 1
Outputs:
- updated: float32 [1152, 128, 1024], P('group', None, 'sector')
The draws below stay inside these ranges and needn't reach their ends.
Inputs may be any that keep to these rules, and one draw needn't show every extreme that they name: `assignment`: each component number appears exactly once.
All inputs are finite; a program needn't handle non-finite values. No bound on the sum of `land_mask` on one device may be relied on, other than what follows from the above.
Results may differ from the reference program's by a relative error of at most 0.00007.
Values sent between devices are 32-bit elements; how exact they have to be, the bound alone decides.
A program may use at most 128 MiB of HBM per device.

```python
import math
import jax
import jax.numpy as jnp
from jax import lax

DIRS = 36
FREQ = 32
SUBSTEPS = 6
LAT = 128
COMPS = 1152
LON = 1024


def touch_ends(entries, rng, smallest, top_value):
    longest = entries.shape.index(max(entries.shape))
    spots = []
    for shift in (0, 1):
        where = [jax.random.randint(jax.random.fold_in(rng, axis), (), 0, length) for axis, length in enumerate(entries.shape)]
        where[longest] = (where[longest] + shift) % entries.shape[longest]
        spots.append(tuple(where))
    return entries.at[spots[0]].set(smallest).at[spots[1]].set(top_value)


def block_levels(key, dims, cuts, low, largest):
    def one(axis_at, shards_of):
        heights = jax.random.uniform(jax.random.fold_in(jax.random.fold_in(key, 6), axis_at), (shards_of,), jnp.float32, low / len(cuts), largest / len(cuts))
        return jnp.repeat(jnp.exp(heights), dims[axis_at] // shards_of).reshape((-1,) + (1,) * (len(dims) - axis_at - 1))

    gain = one(*cuts[0])
    for cut in cuts[1:]:
        gain = gain * one(*cut)
    return gain


def noise(key, shape, width, most, cuts=(), dtype=jnp.bfloat16):
    drawn = width * jax.random.normal(key, shape, jnp.float32)
    if cuts:
        drawn = drawn * block_levels(key, shape, cuts, -0.22, 0.18)
    return jnp.clip(drawn, -most, most).astype(dtype)


def setup_inputs(seed: int = 0) -> dict:
    arg_keys = jax.random.split(jax.random.key(seed), 10)
    return {
        "spectrum": jnp.clip(jnp.exp(math.log(2.0) - 2.9957323 * jax.random.uniform(arg_keys[0], (COMPS, LAT, LON), jnp.float32) ** block_levels(arg_keys[0], (COMPS, LAT, LON), ((0, 16), (2, 8)), -0.2, 0.2)), 0.1, 2.0),
        "land_mask": touch_ends((jax.random.randint(arg_keys[1], (LAT, LON), 0, 5) < 4).astype(jnp.int32), jax.random.fold_in(arg_keys[1], 1), 0, 1),
        "wind_field": noise(arg_keys[2], (2, LAT, LON), 0.5, 3.0, ((1, 16), (2, 8)), jnp.float32),
        "assignment": jax.random.permutation(arg_keys[3], COMPS).astype(jnp.int32),
        "courant": jnp.clip(jnp.exp(jax.random.uniform(arg_keys[4], (FREQ,), jnp.float32, math.log(0.3), math.log(0.65))), 0.3, 0.65),
        "growth": jnp.clip(jnp.exp(jax.random.uniform(arg_keys[5], (FREQ,), jnp.float32, math.log(0.1), math.log(0.5))), 0.1, 0.5),
        "whitecap": jnp.clip(jnp.exp(jax.random.uniform(arg_keys[6], (FREQ,), jnp.float32, math.log(0.2), math.log(1.0))), 0.2, 1.0),
        "weights": jnp.clip(jnp.exp(jax.random.uniform(arg_keys[7], (FREQ,), jnp.float32, math.log(0.5), math.log(5.0))), 0.5, 5.0),
        "spread": noise(arg_keys[8], (FREQ, DIRS, DIRS), DIRS ** -0.5, 1.0, (), jnp.float32),
    }


def flow_terms(kinds, courant):
    direction = kinds % DIRS
    frequency = kinds // DIRS
    angles = (direction.astype(jnp.float32) + 0.5) * (2.0 * math.pi / DIRS)
    speeds = courant[frequency]
    latitude = (jnp.arange(LAT).astype(jnp.float32) + 0.5 - LAT / 2) * (math.pi / 2160.0)
    flow_x = speeds[:, None] * jnp.cos(angles)[:, None] / jnp.cos(latitude)[None, :]
    flow_y = speeds * jnp.sin(angles)
    return flow_x, flow_y


def advance(wave_field, flow_x, flow_y, sea_mask):
    east_rate = jnp.maximum(flow_x, 0.0)[:, None]
    west_rate = jnp.maximum(-flow_x, 0.0)[:, None]
    north_rate = jnp.maximum(flow_y, 0.0)
    south_rate = jnp.maximum(-flow_y, 0.0)
    keep_rate = 1.0 - jnp.abs(flow_x)[:, None] - jnp.abs(flow_y)
    for substep in range(SUBSTEPS):
        from_west = jnp.roll(wave_field, 1, axis=1)
        from_east = jnp.roll(wave_field, -1, axis=1)
        from_south = jnp.pad(wave_field[:-1], ((1, 0), (0, 0)))
        from_north = jnp.pad(wave_field[1:], ((0, 1), (0, 0)))
        wave_field = (keep_rate * wave_field + east_rate * from_west + west_rate * from_east
                      + north_rate * from_south + south_rate * from_north) * sea_mask
    return wave_field


def source_tables(assignment, growth, whitecap, weights, spread):
    direction = assignment % DIRS
    frequency = assignment // DIRS
    angles = (direction.astype(jnp.float32) + 0.5) * (2.0 * math.pi / DIRS)
    picked_rows = spread.reshape(FREQ * DIRS, DIRS)[assignment]
    same_freq = (frequency[:, None] == frequency[None, :]).astype(jnp.float32)
    coupling = picked_rows[:, direction] * same_freq
    return (jnp.cos(angles), jnp.sin(angles), growth[frequency], whitecap[frequency],
            weights[frequency], coupling)


def relax(energy, wind_block, sea_row, tables):
    cosine, sine, growth_rows, whitecap_rows, weight_rows, coupling = tables
    loading = jnp.sum(weight_rows[:, None] * energy, axis=0) / COMPS
    drive = cosine[:, None] * wind_block[0][None, :] + sine[:, None] * wind_block[1][None, :]
    exponent = growth_rows[:, None] * jnp.maximum(drive, 0.0) - whitecap_rows[:, None] * (loading / (1.0 + loading))[None, :]
    mixed = jnp.dot(coupling, energy, precision=lax.Precision.HIGHEST)
    return (energy * jnp.exp(exponent) + 0.5 * mixed) * sea_row[None, :]


def reference(spectrum, land_mask, wind_field, assignment, courant, growth, whitecap, weights, spread):
    sea_mask = land_mask.astype(jnp.float32)
    flow_x, flow_y = flow_terms(assignment, courant)
    propagated = lax.map(lambda operand: advance(operand[0], operand[1], operand[2], sea_mask),
                         (spectrum, flow_x, flow_y))
    tables = source_tables(assignment, growth, whitecap, weights, spread)
    rows_first = lax.map(lambda operand: relax(operand[0], operand[1], operand[2], tables),
                         (jnp.moveaxis(propagated, 1, 0), jnp.moveaxis(wind_field, 1, 0), sea_mask))
    return jnp.moveaxis(rows_first, 0, 1)
```

```python
import functools
import math

import jax
import jax.numpy as jnp
import numpy as np
from jax import lax
from jax.experimental import pallas as pl
from jax.experimental.pallas import tpu as pltpu
from jax.sharding import PartitionSpec as P

MESH = pl.DeviceIdType.MESH
DIRS = 36
FREQ = 32
SUBSTEPS = 6
LAT = 128
LANES = 128
EDGE = SUBSTEPS
SLOT = 2 * EDGE
SUB = 8
EARLY = 6
F32 = jnp.float32
BF16 = jnp.bfloat16


def relu(x):
    return jnp.maximum(x, 0.0)


def kernel(n, ns, comps, spec, icos, lm, wind, cprm, sprm, fprm, rmeta, sphl, out,
           x, p, r, acc, cph, cpl, outs, own, te, tw, ter, twr, s, sm, mb, ld, w16,
           load_sem, halo_send, halo_recv, send1, recv1, send2, recv2):
    me = lax.axis_index("group")
    sec = lax.axis_index("sector")
    east, west = lax.rem(sec + 1, ns), lax.rem(sec + ns - 1, ns)
    total = n * comps
    groups = comps // SUB
    block = LAT // n
    span = n * SUB

    def load(g):
        rows = pl.ds(g * SUB * LAT, SUB * LAT)
        return pltpu.make_async_copy(spec.at[rows], x.at[rows], load_sem.at[g])

    for g in range(groups):
        load(g).start()

    barrier = pltpu.get_barrier_semaphore()

    @pl.loop(1, n)
    def _(k):
        pl.semaphore_signal(barrier, inc=1, device_id={"group": lax.rem(me + k, n)}, device_id_type=MESH)

    for side in (east, west):
        pl.semaphore_signal(barrier, inc=1, device_id={"sector": side}, device_id_type=MESH)

    lane = lax.broadcasted_iota(jnp.int32, (SUB, LANES), 1)
    first = lax.rem(lane, SLOT) < EDGE

    @pl.loop(0, LAT // SUB)
    def _(t):
        for i in range(SUB):
            j = t * SUB + i
            mb[j] = jnp.broadcast_to(lm[pl.ds(j, 1), :].astype(F32), (SUB, LANES))

    for g in range(groups):
        load(g).wait()

    @pl.loop(0, LAT // 4)
    def _(t):
        for i in range(4):
            j = t * 4 + i
            packed = pltpu.roll(mb[j], EDGE + SLOT * groups, axis=1)
            for g in range(groups):
                tile = x[pl.ds(g * SUB * LAT + j, SUB, stride=LAT), :]
                tile = pltpu.roll(tile, EDGE + SLOT * g, axis=1)
                packed = jnp.where((lane >= SLOT * g) & (lane < SLOT * (g + 1)), tile, packed)
            own[j] = packed

    half = LAT // 2

    @pl.loop(0, half // 4)
    def _(t):
        for i in range(4):
            j = t * 4 + i
            low, high = own[j], own[j + half]
            te[j] = jnp.where(first, low, pltpu.roll(high, EDGE, axis=1))
            tw[j] = jnp.where(first, pltpu.roll(high, LANES - EDGE, axis=1), low)

    pl.semaphore_wait(barrier, n + 1)

    def halo(src, dst, k, side):
        return pltpu.make_async_remote_copy(
            src_ref=src, dst_ref=dst, send_sem=halo_send.at[k], recv_sem=halo_recv.at[k],
            device_id={"sector": side}, device_id_type=MESH)

    to_east = halo(te, ter, 0, east)
    to_west = halo(tw, twr, 1, west)
    to_east.start()
    to_west.start()

    def sweep(read, write, mask, coefs):
        rate, keep, north, sx, sy = coefs

        def rows(j0, prev, cur, nexts):
            tiles = [prev, cur] + nexts
            for i in range(SUB):
                e = tiles[i + 1]
                fx = jnp.where(sx, pltpu.roll(e, 1, axis=1), pltpu.roll(e, LANES - 1, axis=1))
                fy = jnp.where(sy, tiles[i], tiles[i + 2])
                new = keep * e + north * fy + (rate * icos[j0 + i]) * (fx - e)
                write(j0 + i, new * mask(j0 + i))
            return tiles[SUB], tiles[SUB + 1]

        def body(t, carry):
            j0 = t * SUB
            return rows(j0, *carry, [read(j0 + 1 + i) for i in range(SUB)])

        zero = jnp.zeros((SUB, LANES), F32)
        prev, cur = lax.fori_loop(0, LAT // SUB - 1, body, (zero, read(0)))
        j0 = LAT - SUB
        rows(j0, prev, cur, [read(j0 + 1 + i) for i in range(SUB - 1)] + [zero])

    def spread_columns(ref, start, count):
        tile = ref[pl.ds(start, SUB), :]
        return [jnp.broadcast_to(tile[:, k:k + 1], (SUB, LANES)) for k in range(count)]

    def mask_row(j):
        return mb[j]

    def main(g):
        rate, keep, north, sx, sy = spread_columns(cprm, pl.multiple_of(g * SUB, SUB), 5)
        coefs = (rate, keep, north, sx > 0.0, sy > 0.0)
        mine = pl.ds(pl.multiple_of(g * SUB, SUB), SUB)

        def write(j, v):
            p[j, mine, :] = v

        sweep(lambda j: x[pl.ds(g * SUB * LAT + j, SUB, stride=LAT), :], write, mask_row, coefs)

        @pl.loop(1, SUBSTEPS)
        def _(_k):
            sweep(lambda j: p[j, mine, :], write, mask_row, coefs)

    def shuffle(g, k):
        peer = lax.rem(me + k, n)
        return pltpu.make_async_remote_copy(
            src_ref=p.at[pl.ds(pl.multiple_of(peer * block, block), block), pl.ds(pl.multiple_of(g * SUB, SUB), SUB), :],
            dst_ref=r.at[:, pl.ds(pl.multiple_of(g * span + me * SUB, SUB), SUB), :],
            send_sem=send1.at[g * n + k], recv_sem=recv1.at[g * n + k],
            device_id={"group": peer}, device_id_type=MESH)

    def keep_mine(g):
        return pltpu.make_async_copy(
            p.at[pl.ds(pl.multiple_of(me * block, block), block), pl.ds(pl.multiple_of(g * SUB, SUB), SUB), :],
            r.at[:, pl.ds(pl.multiple_of(g * span + me * SUB, SUB), SUB), :],
            recv1.at[g * n])

    def merge(g):
        (sx,) = spread_columns(cprm, pl.multiple_of(g * SUB, SUB), 4)[3:]
        seam = jnp.where(sx > 0.0, (lane < EDGE).astype(F32), (lane >= LANES - EDGE).astype(F32)) > 0.0
        mine = pl.ds(pl.multiple_of(g * SUB, SUB), SUB)
        shift = LANES - EDGE - SLOT * g

        @pl.loop(0, LAT // SUB)
        def _(t):
            for i in range(SUB):
                j = t * SUB + i
                p[j, mine, :] = jnp.where(seam, pltpu.roll(s[j], shift, axis=1), p[j, mine, :])

        @pl.loop(1, n)
        def _(k):
            shuffle(g, k).start()

        keep_mine(g).start()

    @pl.loop(0, EARLY)
    def _(g):
        main(g)

    to_east.wait_recv()
    to_west.wait_recv()
    scoefs = [sprm[pl.ds(k * SUB, SUB), :] for k in range(5)]
    eastward = scoefs[3] > 0.0
    lastslot = (lane >= SLOT * groups) & (lane < SLOT * (groups + 1))

    def fan(v):
        v1 = jnp.where(lastslot, v, 0.0)
        v2 = v1 + pltpu.roll(v1, LANES - SLOT, axis=1)
        v4 = v2 + pltpu.roll(v2, LANES - 2 * SLOT, axis=1)
        v8 = v4 + pltpu.roll(v4, LANES - 4 * SLOT, axis=1)
        return v8 + pltpu.roll(v2, LANES - 8 * SLOT, axis=1)

    @pl.loop(0, half // 2)
    def _(t):
        for i in range(2):
            j = t * 2 + i
            fe, fw = ter[j], twr[j]
            for row, ve, vw in ((j, fe, fw), (j + half, pltpu.roll(fe, LANES - EDGE, axis=1), pltpu.roll(fw, EDGE, axis=1))):
                o = own[row]
                xe = jnp.where(first, ve, o)
                xw = jnp.where(first, o, vw)
                s[row] = jnp.where(eastward, xe, xw)
                sm[row] = jnp.where(eastward, fan(xe), fan(xw))

    def write_strip(j, v):
        s[j] = v

    @pl.loop(0, SUBSTEPS)
    def _(_k):
        sweep(lambda j: s[j], write_strip, lambda j: sm[j],
              (scoefs[0], scoefs[1], scoefs[2], eastward, scoefs[4] > 0.0))

    @pl.loop(0, EARLY)
    def _(g):
        merge(g)

    @pl.loop(EARLY, groups)
    def _(g):
        main(g)
        merge(g)

    wrow = jnp.broadcast_to(rmeta[2:3, :], (SUB, total))
    whi = wrow.astype(BF16).astype(F32)
    w16[...] = jnp.concatenate([whi, wrow - whi], axis=0).astype(BF16)
    rowid = lax.broadcasted_iota(jnp.int32, (LANES, total), 0).astype(F32)
    colid = lax.broadcasted_iota(jnp.int32, (LANES, total), 1).astype(F32)

    @pl.loop(0, total // LANES)
    def _(t):
        rows = pl.ds(pl.multiple_of(t * LANES, LANES), LANES)
        meta = fprm[rows, :]
        hot = (jnp.broadcast_to(meta[:, 5:6], (LANES, total)) == colid).astype(F32).astype(BF16)
        picked = jnp.dot(hot, sphl[...], preferred_element_type=F32).astype(BF16)
        dirs = jnp.broadcast_to(rmeta[0:1, :], (LANES, total))
        same = jnp.broadcast_to(meta[:, 4:5], (LANES, total)) == jnp.broadcast_to(rmeta[1:2, :], (LANES, total))
        for ref, base in ((cph, 0), (cpl, LANES // 2)):
            pick = (dirs + base == rowid).astype(F32).astype(BF16)
            full = jnp.dot(picked, pick, preferred_element_type=F32)
            ref[rows, :] = jnp.where(same, full, 0.0).astype(BF16)

    for j in range(block):
        ld[j] = jnp.zeros((SUB, LANES), F32)

        @pl.loop(0, total // LANES)
        def _(t):
            acc[j, pl.ds(pl.multiple_of(t * LANES, LANES), LANES), :] = jnp.zeros((LANES, LANES), F32)

    def arrive(g):
        @pl.loop(1, n)
        def _(k):
            shuffle(g, k).wait_recv()

        keep_mine(g).wait()

    def split(jp, ks):
        e = jnp.concatenate([r[2 * jp, ks, :], r[2 * jp + 1, ks, :]], axis=1)
        hi = e.astype(BF16)
        return hi, (e - hi.astype(F32)).astype(BF16)

    def accumulate(jp, rows, ks, hi, lo):
        ch, cl = cph[rows, ks], cpl[rows, ks]
        part = (jnp.dot(ch, hi, preferred_element_type=F32) + jnp.dot(cl, hi, preferred_element_type=F32)
                + jnp.dot(ch, lo, preferred_element_type=F32))
        acc[2 * jp, rows, :] += part[:, :LANES]
        acc[2 * jp + 1, rows, :] += part[:, LANES:]

    def weigh(jp, ks, hi, lo):
        wh = jnp.dot(w16[:, ks], hi, preferred_element_type=F32)
        wl = jnp.dot(w16[:, ks], lo, preferred_element_type=F32)
        part = wh[:SUB] + wh[SUB:] + wl[:SUB]
        ld[2 * jp] += part[:, :LANES]
        ld[2 * jp + 1] += part[:, LANES:]

    chunk = total // 3

    @pl.loop(0, groups // 2)
    def _(b):
        arrive(2 * b)
        arrive(2 * b + 1)
        ks = pl.ds(pl.multiple_of(b * 2 * span, 2 * span), 2 * span)

        @pl.loop(0, block // 2)
        def _(jp):
            hi, lo = split(jp, ks)
            weigh(jp, ks, hi, lo)

            @pl.loop(0, 3)
            def _(m):
                accumulate(jp, pl.ds(pl.multiple_of(m * chunk, chunk), chunk), ks, hi, lo)

    tail = pl.ds((groups - 1) * span, span)
    arrive(groups - 1)

    @pl.loop(0, block // 2)
    def _(jp):
        hi, lo = split(jp, tail)
        weigh(jp, tail, hi, lo)

    for j in range(block):
        loading = ld[j]
        ld[j] = loading / (1.0 + loading)

    def back(d):
        mine = pl.ds(pl.multiple_of(d * comps, SUB), comps)
        return pltpu.make_async_remote_copy(
            src_ref=outs.at[mine], dst_ref=out.at[:, pl.ds(pl.multiple_of(me * block, block), block), :],
            send_sem=send2.at[lax.rem(d - me + n, n)], recv_sem=recv2.at[lax.rem(d - me + n, n)],
            device_id={"group": d}, device_id_type=MESH)

    def back_mine():
        mine = pl.ds(pl.multiple_of(me * comps, SUB), comps)
        return pltpu.make_async_copy(
            outs.at[mine], out.at[:, pl.ds(pl.multiple_of(me * block, block), block), :], recv2.at[0])

    flat = outs.reshape(n * comps * block, LANES)

    def finish(d):
        @pl.loop(0, groups)
        def _(b):
            at = pl.multiple_of(d * comps + b * SUB, SUB)
            grow, cap, cosine, sine = spread_columns(fprm, at, 4)
            for j in range(block):
                e = r[j, pl.ds(pl.multiple_of(b * span + d * SUB, SUB), SUB), :]
                u = jnp.broadcast_to(wind[j:j + 1, :], (SUB, LANES))
                v = jnp.broadcast_to(wind[block + j:block + j + 1, :], (SUB, LANES))
                power = grow * relu(cosine * u + sine * v) - cap * ld[j]
                new = e * jnp.exp(power) + 0.5 * acc[j, pl.ds(at, SUB), :]
                flat[pl.ds(d * comps * block + b * SUB * block + j, SUB, stride=block), :] = new * mb[me * block + j]

    quarter = n // 4
    base = lax.div(me, quarter)

    @pl.loop(0, 4)
    def _(c):
        turn = jnp.where(c == 0, 2, jnp.where(c == 1, 1, jnp.where(c == 2, 3, 0)))
        m = lax.rem(base + turn, 4)
        rows = pl.ds(pl.multiple_of(m * quarter * comps, 16), quarter * comps)

        @pl.loop(0, block // 2)
        def _(jp):
            hi, lo = split(jp, tail)
            accumulate(jp, rows, tail, hi, lo)

        @pl.loop(0, quarter)
        def _(i):
            d = m * quarter + i
            finish(d)

            @pl.when(d != me)
            def _():
                back(d).start()

            @pl.when(d == me)
            def _():
                back_mine().start()

    @pl.loop(0, groups)
    def _(g):
        @pl.loop(1, n)
        def _(k):
            shuffle(g, k).wait_send()

    to_east.wait_send()
    to_west.wait_send()

    @pl.loop(1, n)
    def _(k):
        back(lax.rem(me + k, n)).wait()

    back_mine().wait()


def freq_onehot(frequency):
    return (frequency[:, None] == jnp.arange(FREQ)[None, :]).astype(F32)


def local(n, ns, spectrum, land_mask, wind_field, assignment, courant, growth, whitecap, weights, spread):
    me = lax.axis_index("group")
    comps = spectrum.shape[0]
    total = assignment.shape[0]
    groups = comps // SUB
    block = LAT // n
    direction = assignment % DIRS
    frequency = assignment // DIRS
    angles = (direction.astype(F32) + 0.5) * (2.0 * math.pi / DIRS)
    cosine, sine = jnp.cos(angles), jnp.sin(angles)
    table = jnp.stack((growth, whitecap, weights, courant), axis=1)
    picked = jnp.dot(freq_onehot(frequency), table, precision=lax.Precision.HIGHEST)
    fprm = jnp.stack((picked[:, 0], picked[:, 1], cosine, sine, frequency.astype(F32), assignment.astype(F32)), axis=1)
    fprm = jnp.pad(fprm, ((0, 0), (0, LANES - fprm.shape[1])))
    order = jnp.stack((direction.astype(F32), frequency.astype(F32), picked[:, 2] / total))
    rmeta = order.reshape(3, n, groups, SUB).transpose(0, 2, 1, 3).reshape(3, total)
    rmeta = jnp.pad(rmeta, ((0, SUB - 3), (0, 0)))
    fx = picked[:, 3] * cosine
    fy = picked[:, 3] * sine
    mine = jnp.stack((jnp.abs(fx), 1.0 - jnp.abs(fy), jnp.abs(fy), (fx > 0.0).astype(F32), (fy > 0.0).astype(F32)), axis=1)
    mine = lax.dynamic_slice_in_dim(mine, me * comps, comps, 0)
    cprm = jnp.pad(mine, ((0, 0), (0, LANES - 5)))
    sprm = jnp.repeat(mine.reshape(groups, SUB, 5).transpose(2, 1, 0), SLOT, axis=2)
    sprm = jnp.pad(sprm, ((0, 0), (0, 0), (0, LANES - groups * SLOT))).reshape(5 * SUB, LANES)
    rows = spread.reshape(FREQ * DIRS, DIRS)
    high = rows.astype(BF16)
    low = (rows - high.astype(F32)).astype(BF16)
    side = ((0, 0), (0, LANES // 2 - DIRS))
    sphl = jnp.concatenate((jnp.pad(high, side), jnp.pad(low, side)), axis=1)
    latitude = (np.arange(LAT, dtype=np.float64) + 0.5 - LAT / 2) * (math.pi / 2160.0)
    icos = jnp.asarray((1.0 / np.cos(latitude)).astype(np.float32))

    vmem = pl.BlockSpec(memory_space=pltpu.VMEM)
    tiles = lambda count: pltpu.VMEM((count, SUB, LANES), F32)
    dma = pltpu.SemaphoreType.DMA
    call = pl.pallas_call(
        functools.partial(kernel, n, ns, comps),
        out_shape=jax.ShapeDtypeStruct((comps, LAT, LANES), F32),
        in_specs=[pl.BlockSpec(memory_space=pl.ANY), pl.BlockSpec(memory_space=pltpu.SMEM)] + [vmem] * 7,
        out_specs=vmem,
        scratch_shapes=[
            pltpu.VMEM((comps * LAT, LANES), F32),
            pltpu.VMEM((LAT, comps, LANES), F32),
            pltpu.VMEM((block, total, LANES), F32),
            pltpu.VMEM((block, total, LANES), F32),
            pltpu.VMEM((total, total), BF16),
            pltpu.VMEM((total, total), BF16),
            pltpu.VMEM((n * comps, block, LANES), F32),
            tiles(LAT), tiles(LAT // 2), tiles(LAT // 2), tiles(LAT // 2), tiles(LAT // 2),
            tiles(LAT), tiles(LAT), tiles(LAT), tiles(block),
            pltpu.VMEM((2 * SUB, total), BF16),
            dma((groups,)), dma((2,)), dma((2,)),
            dma((groups * n,)), dma((groups * n,)), dma((n,)), dma((n,)),
        ],
        compiler_params=pltpu.CompilerParams(collective_id=0, has_side_effects=True, vmem_limit_bytes=56 << 20),
    )
    return call(spectrum.reshape(comps * LAT, LANES), icos, land_mask, wind_field.reshape(2 * block, LANES),
                cprm, sprm, fprm, rmeta, sphl)


def solution(mesh):
    in_specs = (P("group", None, "sector"), P(None, "sector"), P(None, "group", "sector"), P(), P(), P(), P(), P(), P())
    return jax.shard_map(functools.partial(local, mesh.shape["group"], mesh.shape["sector"]), mesh=mesh,
                         in_specs=in_specs, out_specs=P("group", None, "sector"), check_vma=False)
```

```python
import functools
import math

import jax
import jax.numpy as jnp
import numpy as np
from jax import lax
from jax.experimental import pallas as pl
from jax.experimental.pallas import tpu as pltpu
from jax.sharding import PartitionSpec as P

MESH = pl.DeviceIdType.MESH
DIRS = 36
FREQ = 32
SUBSTEPS = 6
LAT = 128
LANES = 128
EDGE = SUBSTEPS
SLOT = 2 * EDGE
SUB = 8
EARLY = 3
HALVES = 2
PARTS = 4
DEEP = 64
F32 = jnp.float32
BF16 = jnp.bfloat16


def relu(x):
    return jnp.maximum(x, 0.0)


def kernel(n, ns, comps, spec, icos, lm, wind, asg, tabs, sp, out,
           x, p, r, acc, cph, cpl, outs, own, te, tw, ter, twr, s, sm, mb, ld, w16,
           kcol, kq, cpar, spar, fpar, spx,
           land, stage,
           load_sem, halo_send, halo_recv, send1, recv1, mine1, send2, recv2, done):
    me = lax.axis_index("group")
    sec = lax.axis_index("sector")
    east, west = lax.rem(sec + 1, ns), lax.rem(sec + ns - 1, ns)
    total = n * comps
    groups = comps // SUB
    block = LAT // n
    span = n * SUB

    def load(g):
        rows = pl.ds(g * SUB * LAT, SUB * LAT)
        return pltpu.make_async_copy(spec.at[rows], x.at[rows], load_sem.at[g])

    for g in range(groups):
        load(g).start()

    barrier = pltpu.get_barrier_semaphore()

    @pl.loop(1, n)
    def _(k):
        pl.semaphore_signal(barrier, inc=1, device_id={"group": lax.rem(me + k, n)}, device_id_type=MESH)

    for side in (east, west):
        pl.semaphore_signal(barrier, inc=1, device_id={"sector": side}, device_id_type=MESH)

    lane = lax.broadcasted_iota(jnp.int32, (SUB, LANES), 1)
    first = lax.rem(lane, SLOT) < EDGE

    @pl.loop(0, LAT // SUB)
    def _(t):
        for i in range(SUB):
            j = t * SUB + i
            mb[j] = jnp.broadcast_to(lm[pl.ds(j, 1), :].astype(F32), (SUB, LANES))

    @pl.loop(0, total // LANES)
    def _(t):
        row = asg[pl.ds(t, 1), :].astype(F32)
        kcol[pl.ds(pl.multiple_of(t * LANES, LANES), LANES), :] = jnp.broadcast_to(row, (LANES, LANES)).T

    def parts(kind):
        freq = jnp.floor((kind + 0.5) * (1.0 / DIRS))
        return kind - DIRS * freq, freq

    lanef = lane.astype(F32)

    def look(k, index):
        hit = jnp.where(lanef == index, jnp.broadcast_to(tabs[k:k + 1, :], (SUB, LANES)), 0.0)
        return jnp.broadcast_to(jnp.sum(hit, axis=1, keepdims=True), (SUB, LANES))

    strips = [jnp.zeros((SUB, LANES), F32)] * 5
    for g in range(groups):
        direction, freq = parts(kcol[pl.ds(pl.multiple_of(me * comps + g * SUB, SUB), SUB), :])
        speed = look(0, freq)
        fx = speed * look(4, direction)
        fy = speed * look(5, direction)
        values = (jnp.abs(fx), 1.0 - jnp.abs(fy), jnp.abs(fy), (fx > 0.0).astype(F32), (fy > 0.0).astype(F32))
        slot = (lane >= SLOT * g) & (lane < SLOT * (g + 1))
        for k in range(5):
            cpar[g * 5 + k] = values[k]
            strips[k] = jnp.where(slot, values[k], strips[k])
    for k in range(5):
        spar[k] = strips[k]

    for g in range(groups):
        load(g).wait()

    half = LAT // 2

    def window(j):
        packed = pltpu.roll(mb[j], EDGE + SLOT * groups, axis=1)
        for g in range(groups):
            tile = x[pl.ds(g * SUB * LAT + j, SUB, stride=LAT), :]
            tile = pltpu.roll(tile, EDGE + SLOT * g, axis=1)
            packed = jnp.where((lane >= SLOT * g) & (lane < SLOT * (g + 1)), tile, packed)
        return packed

    piece = half // PARTS

    def halo(src, dst, k, c, side):
        rows = pl.ds(c * piece, piece)
        return pltpu.make_async_remote_copy(
            src_ref=src.at[rows], dst_ref=dst.at[rows], send_sem=halo_send.at[k * PARTS + c],
            recv_sem=halo_recv.at[k * PARTS + c], device_id={"sector": side}, device_id_type=MESH)

    def to_east(c):
        return halo(te, ter, 0, c, east)

    def to_west(c):
        return halo(tw, twr, 1, c, west)

    @pl.loop(0, half // 4)
    def _(t):
        rows = [t * 4 + i for i in range(4)]
        lows = [window(j) for j in rows]
        highs = [window(j + half) for j in rows]
        for j, low, high in zip(rows, lows, highs):
            own[j] = low
            own[j + half] = high
            te[j] = jnp.where(first, low, pltpu.roll(high, EDGE, axis=1))
            tw[j] = jnp.where(first, pltpu.roll(high, LANES - EDGE, axis=1), low)

    pl.semaphore_wait(barrier, n + 1)

    @pl.loop(0, PARTS)
    def _(c):
        to_east(c).start()
        to_west(c).start()

    def sweep(read, write, mask, coefs):
        rate, keep, north, sx, sy = coefs

        def rows(j0, prev, cur, nexts):
            tiles = [prev, cur] + nexts
            for i in range(DEEP):
                e = tiles[i + 1]
                fx = jnp.where(sx, pltpu.roll(e, 1, axis=1), pltpu.roll(e, LANES - 1, axis=1))
                fy = jnp.where(sy, tiles[i], tiles[i + 2])
                new = keep * e + north * fy + (rate * icos[j0 + i]) * (fx - e)
                write(j0 + i, new * mask(j0 + i))
            return tiles[DEEP], tiles[DEEP + 1]

        def body(t, carry):
            j0 = t * DEEP
            return rows(j0, *carry, [read(j0 + 1 + i) for i in range(DEEP)])

        zero = jnp.zeros((SUB, LANES), F32)
        prev, cur = lax.fori_loop(0, LAT // DEEP - 1, body, (zero, read(0)))
        j0 = LAT - DEEP
        rows(j0, prev, cur, [read(j0 + 1 + i) for i in range(DEEP - 1)] + [zero])

    def mask_row(j):
        return mb[j]

    def main(g):
        rate, keep, north, sx, sy = [cpar[g * 5 + k] for k in range(5)]
        coefs = (rate, keep, north, sx > 0.0, sy > 0.0)
        mine = pl.ds(pl.multiple_of(g * SUB, SUB), SUB)

        def write(j, v):
            p[j, mine, :] = v

        sweep(lambda j: x[pl.ds(g * SUB * LAT + j, SUB, stride=LAT), :], write, mask_row, coefs)

        @pl.loop(1, SUBSTEPS)
        def _(_k):
            sweep(lambda j: p[j, mine, :], write, mask_row, coefs)

    part = block // HALVES

    def source(g, h, peer):
        return p.at[pl.ds(peer * block + h * part, part), pl.ds(pl.multiple_of(g * SUB, SUB), SUB), :]

    def target(g, h):
        return r.at[pl.ds(h * part, part), pl.ds(pl.multiple_of(g * span + me * SUB, SUB), SUB), :]

    def shuffle(g, h):
        @pl.loop(1, n)
        def _(k):
            peer = lax.rem(me + k, n)
            pltpu.make_async_remote_copy(
                src_ref=source(g, h, peer), dst_ref=target(g, h), send_sem=send1.at[g * HALVES + h],
                recv_sem=recv1.at[g * HALVES + h], device_id={"group": peer}, device_id_type=MESH).start()

        keep_mine(g, h).start()

    def keep_mine(g, h):
        return pltpu.make_async_copy(source(g, h, me), target(g, h), mine1.at[g * HALVES + h])

    def whole(g, h):
        view = r.at[pl.ds(h * part, part), pl.ds(pl.multiple_of(g * span, SUB), span - SUB), :]
        return pltpu.make_async_remote_copy(
            src_ref=view, dst_ref=view, send_sem=send1.at[g * HALVES + h], recv_sem=recv1.at[g * HALVES + h],
            device_id={"group": lax.rem(me + 1, n)}, device_id_type=MESH)

    def arrive(g, h):
        whole(g, h).wait_recv()
        keep_mine(g, h).wait()

    def merge(g):
        seam = jnp.where(cpar[g * 5 + 3] > 0.0, (lane < EDGE).astype(F32), (lane >= LANES - EDGE).astype(F32)) > 0.0
        mine = pl.ds(pl.multiple_of(g * SUB, SUB), SUB)
        shift = LANES - EDGE - SLOT * g

        @pl.loop(0, LAT // SUB)
        def _(t):
            for i in range(SUB):
                j = t * SUB + i
                p[j, mine, :] = jnp.where(seam, pltpu.roll(s[j], shift, axis=1), p[j, mine, :])

        shuffle(g, 0)

    @pl.loop(0, EARLY)
    def _(g):
        main(g)

    scoefs = [spar[k] for k in range(5)]
    eastward = scoefs[3] > 0.0
    lastslot = (lane >= SLOT * groups) & (lane < SLOT * (groups + 1))

    def fan(v):
        v1 = jnp.where(lastslot, v, 0.0)
        v2 = v1 + pltpu.roll(v1, LANES - SLOT, axis=1)
        v4 = v2 + pltpu.roll(v2, LANES - 2 * SLOT, axis=1)
        v8 = v4 + pltpu.roll(v4, LANES - 4 * SLOT, axis=1)
        return v8 + pltpu.roll(v2, LANES - 8 * SLOT, axis=1)

    @pl.loop(0, PARTS)
    def _(c):
        to_east(c).wait_recv()
        to_west(c).wait_recv()

        @pl.loop(0, piece // 8)
        def _(t):
            for i in range(8):
                j = c * piece + t * 8 + i
                fe, fw = ter[j], twr[j]
                for row, ve, vw in ((j, fe, fw), (j + half, pltpu.roll(fe, LANES - EDGE, axis=1), pltpu.roll(fw, EDGE, axis=1))):
                    o = own[row]
                    xe = jnp.where(first, ve, o)
                    xw = jnp.where(first, o, vw)
                    s[row] = jnp.where(eastward, xe, xw)
                    sm[row] = jnp.where(eastward, fan(xe), fan(xw))

    def write_strip(j, v):
        s[j] = v

    @pl.loop(0, SUBSTEPS)
    def _(_k):
        sweep(lambda j: s[j], write_strip, lambda j: sm[j],
              (scoefs[0], scoefs[1], scoefs[2], eastward, scoefs[4] > 0.0))

    @pl.loop(0, EARLY)
    def _(g):
        merge(g)
        shuffle(g, 1)

    @pl.loop(EARLY, groups)
    def _(g):
        main(g)
        merge(g)

    @pl.loop(0, total // SUB)
    def _(t):
        at = pl.ds(pl.multiple_of(t * SUB, SUB), SUB)
        direction, freq = parts(kcol[at, :])
        for k, value in enumerate((look(1, freq), look(2, freq), look(4, direction), look(5, direction))):
            fpar[k, at, :] = value

    for g in range(groups):
        column = jnp.concatenate(
            [kcol[pl.ds(d * comps + g * SUB, SUB), :] for d in range(n)], axis=0)
        kq[:, g * LANES:(g + 1) * LANES] = column.T[:SUB]

    dirq, freqq = parts(kq[...])
    rowid = lax.broadcasted_iota(jnp.int32, (LANES, total), 0).astype(F32)
    colid = lax.broadcasted_iota(jnp.int32, (LANES, total), 1).astype(F32)

    def one_hot(hit):
        return hit.astype(F32).astype(BF16)

    share = tabs[...] * (1.0 / total)
    high = share.astype(BF16).astype(F32)
    both = jnp.concatenate([high, share - high], axis=0).astype(BF16)
    picked = jnp.dot(both, one_hot(jnp.broadcast_to(freqq[0:1], (LANES, total)) == rowid), preferred_element_type=F32)
    w16[...] = jnp.concatenate([jnp.broadcast_to(picked[3:4], (SUB, total)),
                                jnp.broadcast_to(picked[SUB + 3:SUB + 4], (SUB, total))], axis=0).astype(BF16)

    spx[...] = jnp.zeros_like(spx)
    spx[:, 0:DIRS] = sp[...]

    @pl.loop(0, total // LANES)
    def _(t):
        rows = pl.ds(pl.multiple_of(t * LANES, LANES), LANES)
        direction, freq = parts(kcol[rows, :])
        hot = one_hot(jnp.concatenate([direction * FREQ + freq] * (total // LANES), axis=1) == colid)
        same = jnp.concatenate([freq] * (total // LANES), axis=1) == jnp.broadcast_to(freqq[0:1], (LANES, total))
        pick = one_hot(jnp.broadcast_to(dirq[0:1], (LANES, total)) == rowid)
        full = spx[...]
        upper = full.astype(BF16)
        lower = (full - upper.astype(F32)).astype(BF16)
        for ref, table in ((cph, upper), (cpl, lower)):
            chosen = jnp.dot(hot, table, preferred_element_type=F32).astype(BF16)
            wide = jnp.dot(chosen, pick, preferred_element_type=F32)
            ref[rows, :] = jnp.where(same, wide, 0.0).astype(BF16)

    for j in range(block):
        ld[j] = jnp.zeros((SUB, LANES), F32)

        @pl.loop(0, total // LANES)
        def _(t):
            acc[j, pl.ds(pl.multiple_of(t * LANES, LANES), LANES), :] = jnp.zeros((LANES, LANES), F32)

    @pl.loop(EARLY, groups)
    def _(g):
        shuffle(g, 1)

    def split(jp, ks):
        e = jnp.concatenate([r[2 * jp, ks, :], r[2 * jp + 1, ks, :]], axis=1)
        hi = e.astype(BF16)
        return hi, (e - hi.astype(F32)).astype(BF16)

    def accumulate(jp, rows, ks, hi, lo):
        ch, cl = cph[rows, ks], cpl[rows, ks]
        part = (jnp.dot(ch, hi, preferred_element_type=F32) + jnp.dot(cl, hi, preferred_element_type=F32)
                + jnp.dot(ch, lo, preferred_element_type=F32))
        acc[2 * jp, rows, :] += part[:, :LANES]
        acc[2 * jp + 1, rows, :] += part[:, LANES:]

    def weigh(jp, ks, hi, lo):
        wh = jnp.dot(w16[:, ks], hi, preferred_element_type=F32)
        wl = jnp.dot(w16[:, ks], lo, preferred_element_type=F32)
        part = wh[:SUB] + wh[SUB:] + wl[:SUB]
        ld[2 * jp] += part[:, :LANES]
        ld[2 * jp + 1] += part[:, LANES:]

    chunk = total // 3

    tail = pl.ds((groups - 1) * span, span)
    quarter = n // 4
    base = lax.div(me, quarter)
    landed = lambda q, h: pl.ds(q * block + h * part, part)

    def sent(h, d):
        return outs.at[pl.ds((h * n + d) * part, part)]

    def back(h, d):
        k = h * n + lax.rem(d - me + n, n)
        return pltpu.make_async_remote_copy(
            src_ref=sent(h, d), dst_ref=land.at[landed(me, h)], send_sem=send2.at[k], recv_sem=recv2.at[k],
            device_id={"group": d}, device_id_type=MESH)

    def back_mine(h):
        return pltpu.make_async_copy(sent(h, me), land.at[landed(me, h)], recv2.at[h * n])

    def finish(h, d):
        @pl.loop(0, groups // 3)
        def _(t):
            for i in range(3):
                b = t * 3 + i
                at = pl.multiple_of(d * comps + b * SUB, SUB)
                grow, cap, cosine, sine = [fpar[k, pl.ds(at, SUB), :] for k in range(4)]
                for jr in range(part):
                    j = h * part + jr
                    e = r[j, pl.ds(pl.multiple_of(b * span + d * SUB, SUB), SUB), :]
                    u = jnp.broadcast_to(wind[pl.ds(j, 1), :], (SUB, LANES))
                    v = jnp.broadcast_to(wind[pl.ds(block + j, 1), :], (SUB, LANES))
                    power = grow * relu(cosine * u + sine * v) - cap * ld[j]
                    new = e * jnp.exp(power) + 0.5 * acc[j, pl.ds(at, SUB), :]
                    outs[(h * n + d) * part + jr, pl.ds(pl.multiple_of(b * SUB, SUB), SUB), :] = new * mb[me * block + j]

    def turn(c):
        return jnp.where(c == 0, 2, jnp.where(c == 1, 1, jnp.where(c == 2, 3, 0)))

    @pl.loop(0, HALVES)
    def _(h):
        pairs = part // 2

        @pl.loop(0, groups // 2)
        def _(b):
            arrive(2 * b, h)
            arrive(2 * b + 1, h)
            ks = pl.ds(pl.multiple_of(b * 2 * span, 2 * span), 2 * span)

            @pl.loop(0, pairs)
            def _(i):
                jp = h * pairs + i
                hi, lo = split(jp, ks)
                weigh(jp, ks, hi, lo)

                @pl.loop(0, 3)
                def _(m):
                    accumulate(jp, pl.ds(pl.multiple_of(m * chunk, chunk), chunk), ks, hi, lo)

        arrive(groups - 1, h)

        @pl.loop(0, pairs)
        def _(i):
            jp = h * pairs + i
            hi, lo = split(jp, tail)
            weigh(jp, tail, hi, lo)

        for jr in range(part):
            j = h * part + jr
            loading = ld[j]
            ld[j] = loading / (1.0 + loading)

        @pl.loop(0, 4)
        def _(c):
            m = lax.rem(base + turn(c), 4)
            rows = pl.ds(pl.multiple_of(m * quarter * comps, 16), quarter * comps)

            @pl.loop(0, pairs)
            def _(i):
                jp = h * pairs + i
                hi, lo = split(jp, tail)
                accumulate(jp, rows, tail, hi, lo)

            @pl.loop(0, quarter)
            def _(i):
                d = m * quarter + i
                finish(h, d)

                @pl.when(d != me)
                def _():
                    back(h, d).start()

                @pl.when(d == me)
                def _():
                    back_mine(h).start()

    @pl.loop(0, groups)
    def _(g):
        for h in range(HALVES):
            whole(g, h).wait_send()

    @pl.loop(0, PARTS)
    def _(c):
        to_east(c).wait_send()
        to_west(c).wait_send()

    flat = stage.reshape(n * comps * block, LANES)

    def deliver(q):
        return pltpu.make_async_copy(
            stage.at[pl.ds(pl.multiple_of(q * comps, SUB), comps)],
            out.at[:, pl.ds(pl.multiple_of(q * block, block), block), :], done.at[q])

    def relayout(q):
        @pl.loop(0, groups // 3)
        def _(t):
            for i in range(3):
                b = t * 3 + i
                for j in range(block):
                    flat[pl.ds((q * comps + b * SUB) * block + j, SUB, stride=block), :] = (
                        land[q * block + j, pl.ds(pl.multiple_of(b * SUB, SUB), SUB), :])

        deliver(q).start()

    @pl.loop(0, 4)
    def _(c):
        m = lax.rem(base + 4 - turn(c), 4)

        @pl.loop(0, quarter)
        def _(i):
            q = m * quarter + i
            k = lax.rem(me - q + n, n)

            @pl.when(q != me)
            def _():
                for h in range(HALVES):
                    back(h, lax.rem(me + k, n)).wait_recv()

            @pl.when(q == me)
            def _():
                for h in range(HALVES):
                    back_mine(h).wait()

            relayout(q)

    @pl.loop(1, n)
    def _(k):
        for h in range(HALVES):
            back(h, lax.rem(me + k, n)).wait_send()

    @pl.loop(0, n)
    def _(q):
        deliver(q).wait()


def local(n, ns, spectrum, land_mask, wind_field, assignment, courant, growth, whitecap, weights, spread):
    comps = spectrum.shape[0]
    total = assignment.shape[0]
    groups = comps // SUB
    block = LAT // n
    turns = np.zeros((4, LANES), np.float32)
    angles = (np.arange(DIRS) + 0.5) * (2.0 * math.pi / DIRS)
    turns[0, :DIRS] = np.cos(angles)
    turns[1, :DIRS] = np.sin(angles)
    tables = jnp.pad(jnp.stack((courant, growth, whitecap, weights)), ((0, 0), (0, LANES - FREQ)))
    tabs = jnp.concatenate((tables, jnp.asarray(turns)))
    latitude = (np.arange(LAT, dtype=np.float64) + 0.5 - LAT / 2) * (math.pi / 2160.0)
    icos = jnp.asarray((1.0 / np.cos(latitude)).astype(np.float32))

    vmem = pl.BlockSpec(memory_space=pltpu.VMEM)
    tiles = lambda count: pltpu.VMEM((count, SUB, LANES), F32)
    dma = pltpu.SemaphoreType.DMA
    call = pl.pallas_call(
        functools.partial(kernel, n, ns, comps),
        out_shape=jax.ShapeDtypeStruct((comps, LAT, LANES), F32),
        in_specs=[pl.BlockSpec(memory_space=pltpu.HBM), pl.BlockSpec(memory_space=pltpu.SMEM)] + [vmem] * 5,
        out_specs=pl.BlockSpec(memory_space=pl.ANY),
        scratch_shapes=[
            pltpu.VMEM((comps * LAT, LANES), F32),
            pltpu.VMEM((LAT, comps, LANES), F32),
            pltpu.VMEM((block, total, LANES), F32),
            pltpu.VMEM((block, total, LANES), F32),
            pltpu.VMEM((total, total), BF16),
            pltpu.VMEM((total, total), BF16),
            pltpu.VMEM((n * block, comps, LANES), F32),
            tiles(LAT), tiles(LAT // 2), tiles(LAT // 2), tiles(LAT // 2), tiles(LAT // 2),
            tiles(LAT), tiles(LAT), tiles(LAT), tiles(block),
            pltpu.VMEM((2 * SUB, total), BF16),
            pltpu.VMEM((total, LANES), F32),
            pltpu.VMEM((SUB, total), F32),
            tiles(groups * 5), tiles(5),
            pltpu.VMEM((4, total, LANES), F32),
            pltpu.VMEM((total, LANES), F32),
            pltpu.VMEM((LAT, comps, LANES), F32),
            pltpu.VMEM((n * comps, block, LANES), F32),
            dma((groups,)), dma((2 * PARTS,)), dma((2 * PARTS,)),
            dma((groups * HALVES,)), dma((groups * HALVES,)), dma((groups * HALVES,)),
            dma((HALVES * n,)), dma((HALVES * n,)), dma((n,)),
        ],
        compiler_params=pltpu.CompilerParams(collective_id=0, has_side_effects=True, vmem_limit_bytes=48 << 20),
    )
    return call(spectrum.reshape(comps * LAT, LANES), icos, land_mask, wind_field.reshape(2 * block, LANES),
                assignment.reshape(total // LANES, LANES), tabs, spread.transpose(1, 0, 2).reshape(FREQ * DIRS, DIRS))


def solution(mesh):
    in_specs = (P("group", None, "sector"), P(None, "sector"), P(None, "group", "sector"), P(), P(), P(), P(), P(), P())
    return jax.shard_map(functools.partial(local, mesh.shape["group"], mesh.shape["sector"]), mesh=mesh,
                         in_specs=in_specs, out_specs=P("group", None, "sector"), check_vma=False)
```

```python
import functools
import math

import jax
import jax.numpy as jnp
import numpy as np
from jax import lax
from jax.experimental import pallas as pl
from jax.experimental.pallas import tpu as pltpu
from jax.sharding import PartitionSpec as P

MESH = pl.DeviceIdType.MESH
DIRS = 36
FREQ = 32
SUBSTEPS = 6
LAT = 128
LANES = 128
EDGE = SUBSTEPS
SLOT = 2 * EDGE
SUB = 8
EARLY = 3
HALVES = 2
PARTS = 3
DEEP = 64
F32 = jnp.float32
BF16 = jnp.bfloat16


def relu(x):
    return jnp.maximum(x, 0.0)


def kernel(n, ns, comps, spec, small, sp, out,
           x, p, r, acc, cph, cpl, outs, own, te, tw, ter, twr, s, sm, mb, ld, w16, icos,
           kcol, kq, cpar, spar, fpar, spx,
           land, stage,
           load_sem, halo_send, halo_recv, send1, recv1, mine1, send2, recv2, done):
    lm = small.at[pl.ds(0, LAT)]
    wind = small.at[pl.ds(LAT, 2 * SUB)]
    tabs = small.at[pl.ds(LAT + 2 * SUB, SUB)]
    asg = small.at[pl.ds(LAT + 3 * SUB, n)]
    me = lax.axis_index("group")
    sec = lax.axis_index("sector")
    east, west = lax.rem(sec + 1, ns), lax.rem(sec + ns - 1, ns)
    total = n * comps
    groups = comps // SUB
    block = LAT // n
    span = n * SUB

    def load(g):
        rows = pl.ds(g * SUB * LAT, SUB * LAT)
        return pltpu.make_async_copy(spec.at[rows], x.at[rows], load_sem.at[g])

    for g in range(groups):
        load(g).start()

    for j in range(LAT):
        icos[j] = np.float32(1.0 / math.cos((j + 0.5 - LAT / 2) * (math.pi / 2160.0)))

    barrier = pltpu.get_barrier_semaphore()

    @pl.loop(1, n)
    def _(k):
        pl.semaphore_signal(barrier, inc=1, device_id={"group": lax.rem(me + k, n)}, device_id_type=MESH)

    for side in (east, west):
        pl.semaphore_signal(barrier, inc=1, device_id={"sector": side}, device_id_type=MESH)

    lane = lax.broadcasted_iota(jnp.int32, (SUB, LANES), 1)
    first = lax.rem(lane, SLOT) < EDGE

    @pl.loop(0, LAT // SUB)
    def _(t):
        for i in range(SUB):
            j = t * SUB + i
            mb[j] = jnp.broadcast_to(lm[pl.ds(j, 1), :], (SUB, LANES))

    @pl.loop(0, total // LANES)
    def _(t):
        row = asg[pl.ds(t, 1), :]
        kcol[pl.ds(pl.multiple_of(t * LANES, LANES), LANES), :] = jnp.broadcast_to(row, (LANES, LANES)).T

    def parts(kind):
        freq = jnp.floor((kind + 0.5) * (1.0 / DIRS))
        return kind - DIRS * freq, freq

    lanef = lane.astype(F32)

    tables = [jnp.broadcast_to(tabs[k:k + 1, :], (SUB, LANES)) for k in range(4)]
    for wave in (math.cos, math.sin):
        values = jnp.zeros((SUB, LANES), F32)
        for d in range(DIRS):
            values = jnp.where(lane == d, np.float32(wave((d + 0.5) * (2.0 * math.pi / DIRS))), values)
        tables.append(values)

    def look(k, index):
        hit = jnp.where(lanef == index, tables[k], 0.0)
        return jnp.broadcast_to(jnp.sum(hit, axis=1, keepdims=True), (SUB, LANES))

    sets = [list(range(EARLY)), list(range(EARLY, groups))]
    strips = [[jnp.zeros((SUB, LANES), F32)] * 5 for _ in sets]
    for g in range(groups):
        which = 0 if g < EARLY else 1
        place = g - sets[which][0]
        direction, freq = parts(kcol[pl.ds(pl.multiple_of(me * comps + g * SUB, SUB), SUB), :])
        speed = look(0, freq)
        fx = speed * look(4, direction)
        fy = speed * look(5, direction)
        values = (jnp.abs(fx), 1.0 - jnp.abs(fy), jnp.abs(fy), (fx > 0.0).astype(F32), (fy > 0.0).astype(F32))
        slot = (lane >= SLOT * place) & (lane < SLOT * (place + 1))
        for k in range(5):
            cpar[g * 5 + k] = values[k]
            strips[which][k] = jnp.where(slot, values[k], strips[which][k])
    for which in range(2):
        for k in range(5):
            spar[which * 5 + k] = strips[which][k]

    for g in range(groups):
        load(g).wait()

    half = LAT // 2
    fourth = half // 2
    fold = SLOT * (EARLY + 1)

    def window(members, j):
        packed = pltpu.roll(mb[j], EDGE + SLOT * len(members), axis=1)
        for i, g in enumerate(members):
            tile = x[pl.ds(g * SUB * LAT + j, SUB, stride=LAT), :]
            tile = pltpu.roll(tile, EDGE + SLOT * i, axis=1)
            packed = jnp.where((lane >= SLOT * i) & (lane < SLOT * (i + 1)), tile, packed)
        return packed

    def pair(which, j):
        low, high = window(sets[which], j), window(sets[which], j + half)
        own[which * LAT + j] = low
        own[which * LAT + j + half] = high
        return (jnp.where(first, low, pltpu.roll(high, EDGE, axis=1)),
                jnp.where(first, pltpu.roll(high, LANES - EDGE, axis=1), low))

    def folded(a, b):
        return jnp.where(lane < fold, a, pltpu.roll(b, fold, axis=1))

    @pl.loop(0, fourth // 4)
    def _(t):
        for i in range(4):
            j = t * 4 + i
            ea, wa = pair(0, j)
            eb, wb = pair(0, j + fourth)
            te[j] = folded(ea, eb)
            tw[j] = folded(wa, wb)

    pl.semaphore_wait(barrier, n + 1)
    starts = [0, fourth, fourth + half // 2, fourth + half]

    def halo(src, dst, k, c, side):
        rows = pl.ds(starts[c], starts[c + 1] - starts[c])
        return pltpu.make_async_remote_copy(
            src_ref=src.at[rows], dst_ref=dst.at[rows], send_sem=halo_send.at[k * PARTS + c],
            recv_sem=halo_recv.at[k * PARTS + c], device_id={"sector": side}, device_id_type=MESH)

    def to_east(c):
        return halo(te, ter, 0, c, east)

    def to_west(c):
        return halo(tw, twr, 1, c, west)

    to_east(0).start()
    to_west(0).start()

    @pl.loop(0, half // 4)
    def _(t):
        for i in range(4):
            j = t * 4 + i
            te[fourth + j], tw[fourth + j] = pair(1, j)

    for c in (1, 2):
        to_east(c).start()
        to_west(c).start()

    def sweep(read, write, mask, coefs):
        rate, keep, north, sx, sy = coefs

        def rows(j0, prev, cur, nexts):
            tiles = [prev, cur] + nexts
            for i in range(DEEP):
                e = tiles[i + 1]
                fx = jnp.where(sx, pltpu.roll(e, 1, axis=1), pltpu.roll(e, LANES - 1, axis=1))
                fy = jnp.where(sy, tiles[i], tiles[i + 2])
                new = keep * e + north * fy + (rate * icos[j0 + i]) * (fx - e)
                write(j0 + i, new * mask(j0 + i))
            return tiles[DEEP], tiles[DEEP + 1]

        def body(t, carry):
            j0 = t * DEEP
            return rows(j0, *carry, [read(j0 + 1 + i) for i in range(DEEP)])

        zero = jnp.zeros((SUB, LANES), F32)
        prev, cur = lax.fori_loop(0, LAT // DEEP - 1, body, (zero, read(0)))
        j0 = LAT - DEEP
        rows(j0, prev, cur, [read(j0 + 1 + i) for i in range(DEEP - 1)] + [zero])

    def mask_row(j):
        return mb[j]

    def main(g):
        rate, keep, north, sx, sy = [cpar[g * 5 + k] for k in range(5)]
        coefs = (rate, keep, north, sx > 0.0, sy > 0.0)
        mine = pl.ds(pl.multiple_of(g * SUB, SUB), SUB)

        def write(j, v):
            p[j, mine, :] = v

        sweep(lambda j: x[pl.ds(g * SUB * LAT + j, SUB, stride=LAT), :], write, mask_row, coefs)

        @pl.loop(1, SUBSTEPS)
        def _(_k):
            sweep(lambda j: p[j, mine, :], write, mask_row, coefs)

    part = block // HALVES

    def source(g, h, peer):
        return p.at[pl.ds(peer * block + h * part, part), pl.ds(pl.multiple_of(g * SUB, SUB), SUB), :]

    def target(g, h):
        return r.at[pl.ds(h * part, part), pl.ds(pl.multiple_of(g * span + me * SUB, SUB), SUB), :]

    def shuffle(g, h):
        @pl.loop(1, n)
        def _(k):
            peer = lax.rem(me + k, n)
            pltpu.make_async_remote_copy(
                src_ref=source(g, h, peer), dst_ref=target(g, h), send_sem=send1.at[g * HALVES + h],
                recv_sem=recv1.at[g * HALVES + h], device_id={"group": peer}, device_id_type=MESH).start()

        keep_mine(g, h).start()

    def keep_mine(g, h):
        return pltpu.make_async_copy(source(g, h, me), target(g, h), mine1.at[g * HALVES + h])

    def whole(g, h):
        view = r.at[pl.ds(h * part, part), pl.ds(pl.multiple_of(g * span, SUB), span - SUB), :]
        return pltpu.make_async_remote_copy(
            src_ref=view, dst_ref=view, send_sem=send1.at[g * HALVES + h], recv_sem=recv1.at[g * HALVES + h],
            device_id={"group": lax.rem(me + 1, n)}, device_id_type=MESH)

    def arrive(g, h):
        whole(g, h).wait_recv()
        keep_mine(g, h).wait()

    def merge(g, origin):
        seam = jnp.where(cpar[g * 5 + 3] > 0.0, (lane < EDGE).astype(F32), (lane >= LANES - EDGE).astype(F32)) > 0.0
        mine = pl.ds(pl.multiple_of(g * SUB, SUB), SUB)
        shift = LANES - EDGE - SLOT * (g - origin)

        @pl.loop(0, LAT // (2 * SUB))
        def _(t):
            for i in range(2 * SUB):
                j = t * 2 * SUB + i
                p[j, mine, :] = jnp.where(seam, pltpu.roll(s[j], shift, axis=1), p[j, mine, :])

        shuffle(g, 0)

    def fan(v, last):
        v1 = jnp.where((lane >= SLOT * last) & (lane < SLOT * (last + 1)), v, 0.0)
        v2 = v1 + pltpu.roll(v1, LANES - SLOT, axis=1)
        v4 = v2 + pltpu.roll(v2, LANES - 2 * SLOT, axis=1)
        return v4 if last < 4 else v4 + pltpu.roll(v4, LANES - 4 * SLOT, axis=1)

    def unpack(which, pairs):
        last = len(sets[which])
        eastward = spar[which * 5 + 3] > 0.0
        for j, fe, fw in pairs:
            for row, ve, vw in ((j, fe, fw), (j + half, pltpu.roll(fe, LANES - EDGE, axis=1), pltpu.roll(fw, EDGE, axis=1))):
                o = own[which * LAT + row]
                xe = jnp.where(first, ve, o)
                xw = jnp.where(first, o, vw)
                s[row] = jnp.where(eastward, xe, xw)
                sm[row] = jnp.where(eastward, fan(xe, last), fan(xw, last))

    def write_strip(j, v):
        s[j] = v

    def strips_of(which):
        scoefs = [spar[which * 5 + k] for k in range(5)]

        @pl.loop(0, SUBSTEPS)
        def _(_k):
            sweep(lambda j: s[j], write_strip, lambda j: sm[j],
                  (scoefs[0], scoefs[1], scoefs[2], scoefs[3] > 0.0, scoefs[4] > 0.0))

    @pl.loop(0, EARLY)
    def _(g):
        main(g)

    to_east(0).wait_recv()
    to_west(0).wait_recv()

    @pl.loop(0, fourth // 4)
    def _(t):
        pairs = []
        for i in range(4):
            j = t * 4 + i
            fe, fw = ter[j], twr[j]
            pairs.append((j, fe, fw))
            pairs.append((j + fourth, pltpu.roll(fe, LANES - fold, axis=1), pltpu.roll(fw, LANES - fold, axis=1)))
        unpack(0, pairs)

    strips_of(0)

    @pl.loop(0, EARLY)
    def _(g):
        merge(g, 0)
        shuffle(g, 1)

    @pl.loop(EARLY, EARLY + 1)
    def _(g):
        main(g)

    for c in (1, 2):
        to_east(c).wait_recv()
        to_west(c).wait_recv()

        @pl.loop(0, half // 16)
        def _(t):
            rows = [(c - 1) * (half // 2) + t * 8 + i for i in range(8)]
            unpack(1, [(j, ter[fourth + j], twr[fourth + j]) for j in rows])

    strips_of(1)
    merge(EARLY, EARLY)

    @pl.loop(EARLY + 1, groups)
    def _(g):
        main(g)
        merge(g, EARLY)

    @pl.loop(EARLY, groups)
    def _(g):
        shuffle(g, 1)

    @pl.loop(0, total // (SUB * SUB))
    def _(t):
        tiles = [pl.ds(pl.multiple_of(t * SUB * SUB + i * SUB, SUB), SUB) for i in range(SUB)]
        kinds = [parts(kcol[at, :]) for at in tiles]
        for at, (direction, freq) in zip(tiles, kinds):
            for k, value in enumerate((look(1, freq), look(2, freq), look(4, direction), look(5, direction))):
                fpar[k, at, :] = value

    for g in range(groups):
        column = jnp.concatenate(
            [kcol[pl.ds(d * comps + g * SUB, SUB), :] for d in range(n)], axis=0)
        kq[:, g * LANES:(g + 1) * LANES] = column.T[:SUB]

    dirq, freqq = parts(kq[...])
    rowid = lax.broadcasted_iota(jnp.int32, (LANES, total), 0).astype(F32)
    colid = lax.broadcasted_iota(jnp.int32, (LANES, total), 1).astype(F32)

    def one_hot(hit):
        return hit.astype(F32).astype(BF16)

    share = tabs[0:SUB, :] * (1.0 / total)
    high = share.astype(BF16).astype(F32)
    both = jnp.concatenate([high, share - high], axis=0).astype(BF16)
    picked = jnp.dot(both, one_hot(jnp.broadcast_to(freqq[0:1], (LANES, total)) == rowid), preferred_element_type=F32)
    w16[...] = jnp.concatenate([jnp.broadcast_to(picked[3:4], (SUB, total)),
                                jnp.broadcast_to(picked[SUB + 3:SUB + 4], (SUB, total))], axis=0).astype(BF16)

    spx[...] = jnp.zeros_like(spx)
    spx[:, 0:DIRS] = sp[...]

    @pl.loop(0, total // LANES)
    def _(t):
        rows = pl.ds(pl.multiple_of(t * LANES, LANES), LANES)
        direction, freq = parts(kcol[rows, :])
        hot = one_hot(jnp.concatenate([direction * FREQ + freq] * (total // LANES), axis=1) == colid)
        same = jnp.concatenate([freq] * (total // LANES), axis=1) == jnp.broadcast_to(freqq[0:1], (LANES, total))
        pick = one_hot(jnp.broadcast_to(dirq[0:1], (LANES, total)) == rowid)
        full = spx[...]
        upper = full.astype(BF16)
        lower = (full - upper.astype(F32)).astype(BF16)
        for ref, table in ((cph, upper), (cpl, lower)):
            chosen = jnp.dot(hot, table, preferred_element_type=F32).astype(BF16)
            wide = jnp.dot(chosen, pick, preferred_element_type=F32)
            ref[rows, :] = jnp.where(same, wide, 0.0).astype(BF16)

    for j in range(block):
        ld[j] = jnp.zeros((SUB, LANES), F32)

        @pl.loop(0, total // LANES)
        def _(t):
            acc[j, pl.ds(pl.multiple_of(t * LANES, LANES), LANES), :] = jnp.zeros((LANES, LANES), F32)

    def split(jp, ks):
        e = jnp.concatenate([r[2 * jp, ks, :], r[2 * jp + 1, ks, :]], axis=1)
        hi = e.astype(BF16)
        return hi, (e - hi.astype(F32)).astype(BF16)

    def accumulate(jp, rows, ks, hi, lo):
        ch, cl = cph[rows, ks], cpl[rows, ks]
        part = (jnp.dot(ch, hi, preferred_element_type=F32) + jnp.dot(cl, hi, preferred_element_type=F32)
                + jnp.dot(ch, lo, preferred_element_type=F32))
        acc[2 * jp, rows, :] += part[:, :LANES]
        acc[2 * jp + 1, rows, :] += part[:, LANES:]

    def weigh(jp, ks, hi, lo):
        wh = jnp.dot(w16[:, ks], hi, preferred_element_type=F32)
        wl = jnp.dot(w16[:, ks], lo, preferred_element_type=F32)
        part = wh[:SUB] + wh[SUB:] + wl[:SUB]
        ld[2 * jp] += part[:, :LANES]
        ld[2 * jp + 1] += part[:, LANES:]

    chunk = total // 3

    tail = pl.ds((groups - 1) * span, span)
    quarter = n // 4
    base = lax.div(me, quarter)
    landed = lambda q, h: pl.ds(q * block + h * part, part)

    def sent(h, d):
        return outs.at[pl.ds((h * n + d) * part, part)]

    def back(h, d):
        k = h * n + lax.rem(d - me + n, n)
        return pltpu.make_async_remote_copy(
            src_ref=sent(h, d), dst_ref=land.at[landed(me, h)], send_sem=send2.at[k], recv_sem=recv2.at[k],
            device_id={"group": d}, device_id_type=MESH)

    def back_mine(h):
        return pltpu.make_async_copy(sent(h, me), land.at[landed(me, h)], recv2.at[h * n])

    def finish(h, d):
        @pl.loop(0, groups // 3)
        def _(t):
            for i in range(3):
                b = t * 3 + i
                at = pl.multiple_of(d * comps + b * SUB, SUB)
                grow, cap, cosine, sine = [fpar[k, pl.ds(at, SUB), :] for k in range(4)]
                for jr in range(part):
                    j = h * part + jr
                    e = r[j, pl.ds(pl.multiple_of(b * span + d * SUB, SUB), SUB), :]
                    u = jnp.broadcast_to(wind[pl.ds(j, 1), :], (SUB, LANES))
                    v = jnp.broadcast_to(wind[pl.ds(block + j, 1), :], (SUB, LANES))
                    power = grow * relu(cosine * u + sine * v) - cap * ld[j]
                    new = e * jnp.exp(power) + 0.5 * acc[j, pl.ds(at, SUB), :]
                    outs[(h * n + d) * part + jr, pl.ds(pl.multiple_of(b * SUB, SUB), SUB), :] = new * mb[me * block + j]

    def turn(c):
        return jnp.where(c == 0, 2, jnp.where(c == 1, 1, jnp.where(c == 2, 3, 0)))

    @pl.loop(0, HALVES)
    def _(h):
        pairs = part // 2

        @pl.loop(0, groups // 2)
        def _(b):
            arrive(2 * b, h)
            arrive(2 * b + 1, h)
            ks = pl.ds(pl.multiple_of(b * 2 * span, 2 * span), 2 * span)

            @pl.loop(0, pairs)
            def _(i):
                jp = h * pairs + i
                hi, lo = split(jp, ks)
                weigh(jp, ks, hi, lo)

                @pl.loop(0, 3)
                def _(m):
                    accumulate(jp, pl.ds(pl.multiple_of(m * chunk, chunk), chunk), ks, hi, lo)

        arrive(groups - 1, h)

        @pl.loop(0, pairs)
        def _(i):
            jp = h * pairs + i
            hi, lo = split(jp, tail)
            weigh(jp, tail, hi, lo)

        for jr in range(part):
            j = h * part + jr
            loading = ld[j]
            ld[j] = loading / (1.0 + loading)

        @pl.loop(0, 4)
        def _(c):
            m = lax.rem(base + turn(c), 4)
            rows = pl.ds(pl.multiple_of(m * quarter * comps, 16), quarter * comps)

            @pl.loop(0, pairs)
            def _(i):
                jp = h * pairs + i
                hi, lo = split(jp, tail)
                accumulate(jp, rows, tail, hi, lo)

            @pl.loop(0, quarter)
            def _(i):
                d = m * quarter + i
                finish(h, d)

                @pl.when(d != me)
                def _():
                    back(h, d).start()

                @pl.when(d == me)
                def _():
                    back_mine(h).start()

    @pl.loop(0, groups)
    def _(g):
        for h in range(HALVES):
            whole(g, h).wait_send()

    for c in range(PARTS):
        to_east(c).wait_send()
        to_west(c).wait_send()

    flat = stage.reshape(n * comps * block, LANES)

    def deliver(q):
        return pltpu.make_async_copy(
            stage.at[pl.ds(pl.multiple_of(q * comps, SUB), comps)],
            out.at[:, pl.ds(pl.multiple_of(q * block, block), block), :], done.at[q])

    def relayout(q):
        @pl.loop(0, groups // 3)
        def _(t):
            for i in range(3):
                b = t * 3 + i
                for j in range(block):
                    flat[pl.ds((q * comps + b * SUB) * block + j, SUB, stride=block), :] = (
                        land[q * block + j, pl.ds(pl.multiple_of(b * SUB, SUB), SUB), :])

        deliver(q).start()

    @pl.loop(0, 4)
    def _(c):
        m = lax.rem(base + 4 - turn(c), 4)

        @pl.loop(0, quarter)
        def _(i):
            q = m * quarter + i
            k = lax.rem(me - q + n, n)

            @pl.when(q != me)
            def _():
                for h in range(HALVES):
                    back(h, lax.rem(me + k, n)).wait_recv()

            @pl.when(q == me)
            def _():
                for h in range(HALVES):
                    back_mine(h).wait()

            relayout(q)

    @pl.loop(1, n)
    def _(k):
        for h in range(HALVES):
            back(h, lax.rem(me + k, n)).wait_send()

    @pl.loop(0, n)
    def _(q):
        deliver(q).wait()


def local(n, ns, spectrum, land_mask, wind_field, assignment, courant, growth, whitecap, weights, spread):
    comps = spectrum.shape[0]
    total = assignment.shape[0]
    groups = comps // SUB
    block = LAT // n
    small = jnp.concatenate((
        land_mask.astype(F32),
        wind_field.reshape(2 * block, LANES),
        jnp.pad(jnp.stack((courant, growth, whitecap, weights)), ((0, SUB - 4), (0, LANES - FREQ))),
        jnp.pad(assignment.astype(F32).reshape(total // LANES, LANES), ((0, n - total // LANES), (0, 0))),
    ))
    vmem = pl.BlockSpec(memory_space=pltpu.VMEM)
    tiles = lambda count: pltpu.VMEM((count, SUB, LANES), F32)
    dma = pltpu.SemaphoreType.DMA
    call = pl.pallas_call(
        functools.partial(kernel, n, ns, comps),
        out_shape=jax.ShapeDtypeStruct((comps, LAT, LANES), F32),
        in_specs=[pl.BlockSpec(memory_space=pl.ANY)] + [vmem] * 2,
        out_specs=pl.BlockSpec(memory_space=pl.ANY),
        scratch_shapes=[
            pltpu.VMEM((comps * LAT, LANES), F32),
            pltpu.VMEM((LAT, comps, LANES), F32),
            pltpu.VMEM((block, total, LANES), F32),
            pltpu.VMEM((block, total, LANES), F32),
            pltpu.VMEM((total, total), BF16),
            pltpu.VMEM((total, total), BF16),
            pltpu.VMEM((n * block, comps, LANES), F32),
            tiles(2 * LAT), tiles(LAT), tiles(LAT), tiles(LAT), tiles(LAT),
            tiles(LAT), tiles(LAT), tiles(LAT), tiles(block),
            pltpu.VMEM((2 * SUB, total), BF16),
            pltpu.SMEM((LAT,), F32),
            pltpu.VMEM((total, LANES), F32),
            pltpu.VMEM((SUB, total), F32),
            tiles(groups * 5), tiles(10),
            pltpu.VMEM((4, total, LANES), F32),
            pltpu.VMEM((total, LANES), F32),
            pltpu.VMEM((LAT, comps, LANES), F32),
            pltpu.VMEM((n * comps, block, LANES), F32),
            dma((groups,)), dma((2 * PARTS,)), dma((2 * PARTS,)),
            dma((groups * HALVES,)), dma((groups * HALVES,)), dma((groups * HALVES,)),
            dma((HALVES * n,)), dma((HALVES * n,)), dma((n,)),
        ],
        compiler_params=pltpu.CompilerParams(collective_id=0, has_side_effects=True, vmem_limit_bytes=48 << 20),
    )
    return call(spectrum.reshape(comps * LAT, LANES), small, spread.transpose(1, 0, 2).reshape(FREQ * DIRS, DIRS))


def solution(mesh):
    in_specs = (P("group", None, "sector"), P(None, "sector"), P(None, "group", "sector"), P(), P(), P(), P(), P(), P())
    return jax.shard_map(functools.partial(local, mesh.shape["group"], mesh.shape["sector"]), mesh=mesh,
                         in_specs=in_specs, out_specs=P("group", None, "sector"), check_vma=False)
```

```python
import functools
import math

import jax
import jax.numpy as jnp
import numpy as np
from jax import lax
from jax.experimental import pallas as pl
from jax.experimental.pallas import tpu as pltpu
from jax.sharding import PartitionSpec as P

MESH = pl.DeviceIdType.MESH
DIRS = 36
FREQ = 32
SUBSTEPS = 6
LAT = 128
LANES = 128
EDGE = SUBSTEPS
SLOT = 2 * EDGE
SUB = 8
EARLY = 2
HALVES = 2
PARTS = 3
DEEP = 64
F32 = jnp.float32
BF16 = jnp.bfloat16


def relu(x):
    return jnp.maximum(x, 0.0)


def kernel(n, ns, comps, spec, whole_small, part_small, sp, out,
           x, p, r, acc, cph, cpl, outs, own, te, tw, ter, twr, s, sm, mb, ld, w16, icos,
           kcol, kq, cpar, spar, fpar, spx,
           land, stage,
           load_sem, halo_send, halo_recv, send1, recv1, mine1, send2, recv2, done):
    lm = whole_small.at[pl.ds(0, LAT)]
    asg = whole_small.at[pl.ds(LAT, n)]
    wind = part_small.at[pl.ds(0, 2 * SUB)]
    tabs = part_small.at[pl.ds(2 * SUB, SUB)]
    me = lax.axis_index("group")
    sec = lax.axis_index("sector")
    east, west = lax.rem(sec + 1, ns), lax.rem(sec + ns - 1, ns)
    total = n * comps
    groups = comps // SUB
    block = LAT // n
    span = n * SUB

    def load(g):
        rows = pl.ds(g * SUB * LAT, SUB * LAT)
        return pltpu.make_async_copy(spec.at[rows], x.at[rows], load_sem.at[g])

    for g in range(groups):
        load(g).start()

    barrier = pltpu.get_barrier_semaphore()

    @pl.loop(1, n)
    def _(k):
        pl.semaphore_signal(barrier, inc=1, device_id={"group": lax.rem(me + k, n)}, device_id_type=MESH)

    for side in (east, west):
        pl.semaphore_signal(barrier, inc=1, device_id={"sector": side}, device_id_type=MESH)

    lane = lax.broadcasted_iota(jnp.int32, (SUB, LANES), 1)
    first = lax.rem(lane, SLOT) < EDGE

    @pl.loop(0, LAT // SUB)
    def _(t):
        for i in range(SUB):
            j = t * SUB + i
            mb[j] = jnp.broadcast_to(lm[pl.ds(j, 1), :].astype(F32), (SUB, LANES))

    sets = [list(range(EARLY)), list(range(EARLY, groups))]
    for g in range(EARLY):
        load(g).wait()

    half = LAT // 2
    fourth = half // 2
    fold = SLOT * (EARLY + 1)

    def window(members, j):
        packed = pltpu.roll(mb[j], EDGE + SLOT * len(members), axis=1)
        for i, g in enumerate(members):
            tile = x[pl.ds(g * SUB * LAT + j, SUB, stride=LAT), :]
            tile = pltpu.roll(tile, EDGE + SLOT * i, axis=1)
            packed = jnp.where((lane >= SLOT * i) & (lane < SLOT * (i + 1)), tile, packed)
        return packed

    def pair(which, j):
        low, high = window(sets[which], j), window(sets[which], j + half)
        own[which * LAT + j] = low
        own[which * LAT + j + half] = high
        return (jnp.where(first, low, pltpu.roll(high, EDGE, axis=1)),
                jnp.where(first, pltpu.roll(high, LANES - EDGE, axis=1), low))

    def folded(a, b):
        return jnp.where(lane < fold, a, pltpu.roll(b, fold, axis=1))

    @pl.loop(0, fourth // 4)
    def _(t):
        for i in range(4):
            j = t * 4 + i
            ea, wa = pair(0, j)
            eb, wb = pair(0, j + fourth)
            te[j] = folded(ea, eb)
            tw[j] = folded(wa, wb)

    pl.semaphore_wait(barrier, n + 1)
    starts = [0, fourth, fourth + half // 2, fourth + half]

    def halo(src, dst, k, c, side):
        rows = pl.ds(starts[c], starts[c + 1] - starts[c])
        return pltpu.make_async_remote_copy(
            src_ref=src.at[rows], dst_ref=dst.at[rows], send_sem=halo_send.at[k * PARTS + c],
            recv_sem=halo_recv.at[k * PARTS + c], device_id={"sector": side}, device_id_type=MESH)

    def to_east(c):
        return halo(te, ter, 0, c, east)

    def to_west(c):
        return halo(tw, twr, 1, c, west)

    to_east(0).start()
    to_west(0).start()

    for g in range(EARLY, groups):
        load(g).wait()

    @pl.loop(0, half // 4)
    def _(t):
        for i in range(4):
            j = t * 4 + i
            te[fourth + j], tw[fourth + j] = pair(1, j)

    for c in (1, 2):
        to_east(c).start()
        to_west(c).start()

    for j in range(LAT):
        icos[j] = np.float32(1.0 / math.cos((j + 0.5 - LAT / 2) * (math.pi / 2160.0)))

    @pl.loop(0, total // LANES)
    def _(t):
        row = asg[pl.ds(t, 1), :].astype(F32)
        kcol[pl.ds(pl.multiple_of(t * LANES, LANES), LANES), :] = jnp.broadcast_to(row, (LANES, LANES)).T

    def parts(kind):
        freq = jnp.floor((kind + 0.5) * (1.0 / DIRS))
        return kind - DIRS * freq, freq

    lanef = lane.astype(F32)

    shared = jnp.broadcast_to(tabs[0:1, :], (SUB, LANES))
    tables = [shared] * 4
    for wave in (math.cos, math.sin):
        values = jnp.zeros((SUB, LANES), F32)
        for d in range(DIRS):
            values = jnp.where(lane == d, np.float32(wave((d + 0.5) * (2.0 * math.pi / DIRS))), values)
        tables.append(values)

    def look(k, index):
        hit = jnp.where(lanef == index + float(FREQ * k) if k < 4 else lanef == index, tables[k], 0.0)
        return jnp.broadcast_to(jnp.sum(hit, axis=1, keepdims=True), (SUB, LANES))

    strips = [[jnp.zeros((SUB, LANES), F32)] * 5 for _ in sets]
    for g in range(groups):
        which = 0 if g < EARLY else 1
        place = g - sets[which][0]
        direction, freq = parts(kcol[pl.ds(pl.multiple_of(me * comps + g * SUB, SUB), SUB), :])
        speed = look(0, freq)
        fx = speed * look(4, direction)
        fy = speed * look(5, direction)
        values = (jnp.abs(fx), 1.0 - jnp.abs(fy), jnp.abs(fy), (fx > 0.0).astype(F32), (fy > 0.0).astype(F32))
        slot = (lane >= SLOT * place) & (lane < SLOT * (place + 1))
        for k in range(5):
            cpar[g * 5 + k] = values[k]
            strips[which][k] = jnp.where(slot, values[k], strips[which][k])
    for which in range(2):
        for k in range(5):
            spar[which * 5 + k] = strips[which][k]

    def sweep(read, write, mask, coefs):
        rate, keep, north, sx, sy = coefs

        def rows(j0, prev, cur, nexts):
            tiles = [prev, cur] + nexts
            for i in range(DEEP):
                e = tiles[i + 1]
                fx = jnp.where(sx, pltpu.roll(e, 1, axis=1), pltpu.roll(e, LANES - 1, axis=1))
                fy = jnp.where(sy, tiles[i], tiles[i + 2])
                new = keep * e + north * fy + (rate * icos[j0 + i]) * (fx - e)
                write(j0 + i, new * mask(j0 + i))
            return tiles[DEEP], tiles[DEEP + 1]

        def body(t, carry):
            j0 = t * DEEP
            return rows(j0, *carry, [read(j0 + 1 + i) for i in range(DEEP)])

        zero = jnp.zeros((SUB, LANES), F32)
        prev, cur = lax.fori_loop(0, LAT // DEEP - 1, body, (zero, read(0)))
        j0 = LAT - DEEP
        rows(j0, prev, cur, [read(j0 + 1 + i) for i in range(DEEP - 1)] + [zero])

    def mask_row(j):
        return mb[j]

    def main(g):
        rate, keep, north, sx, sy = [cpar[g * 5 + k] for k in range(5)]
        coefs = (rate, keep, north, sx > 0.0, sy > 0.0)
        mine = pl.ds(pl.multiple_of(g * SUB, SUB), SUB)

        def write(j, v):
            p[j, mine, :] = v

        sweep(lambda j: x[pl.ds(g * SUB * LAT + j, SUB, stride=LAT), :], write, mask_row, coefs)

        @pl.loop(1, SUBSTEPS)
        def _(_k):
            sweep(lambda j: p[j, mine, :], write, mask_row, coefs)

    part = block // HALVES

    def source(g, h, peer):
        return p.at[pl.ds(peer * block + h * part, part), pl.ds(pl.multiple_of(g * SUB, SUB), SUB), :]

    def target(g, h):
        return r.at[pl.ds(h * part, part), pl.ds(pl.multiple_of(g * span + me * SUB, SUB), SUB), :]

    def shuffle(g, h):
        @pl.loop(1, n)
        def _(k):
            peer = lax.rem(me + k, n)
            pltpu.make_async_remote_copy(
                src_ref=source(g, h, peer), dst_ref=target(g, h), send_sem=send1.at[g * HALVES + h],
                recv_sem=recv1.at[g * HALVES + h], device_id={"group": peer}, device_id_type=MESH).start()

        keep_mine(g, h).start()

    def keep_mine(g, h):
        return pltpu.make_async_copy(source(g, h, me), target(g, h), mine1.at[g * HALVES + h])

    def whole(g, h):
        view = r.at[pl.ds(h * part, part), pl.ds(pl.multiple_of(g * span, SUB), span - SUB), :]
        return pltpu.make_async_remote_copy(
            src_ref=view, dst_ref=view, send_sem=send1.at[g * HALVES + h], recv_sem=recv1.at[g * HALVES + h],
            device_id={"group": lax.rem(me + 1, n)}, device_id_type=MESH)

    def arrive(g, h):
        whole(g, h).wait_recv()
        keep_mine(g, h).wait()

    def merge(g, origin):
        seam = jnp.where(cpar[g * 5 + 3] > 0.0, (lane < EDGE).astype(F32), (lane >= LANES - EDGE).astype(F32)) > 0.0
        mine = pl.ds(pl.multiple_of(g * SUB, SUB), SUB)
        shift = LANES - EDGE - SLOT * (g - origin)

        @pl.loop(0, LAT // (2 * SUB))
        def _(t):
            for i in range(2 * SUB):
                j = t * 2 * SUB + i
                p[j, mine, :] = jnp.where(seam, pltpu.roll(s[j], shift, axis=1), p[j, mine, :])

        shuffle(g, 0)

    def fan(v, last):
        v1 = jnp.where((lane >= SLOT * last) & (lane < SLOT * (last + 1)), v, 0.0)
        v2 = v1 + pltpu.roll(v1, LANES - SLOT, axis=1)
        v4 = v2 + pltpu.roll(v2, LANES - 2 * SLOT, axis=1)
        return v4 if last < 4 else v4 + pltpu.roll(v4, LANES - 4 * SLOT, axis=1)

    def unpack(which, pairs):
        last = len(sets[which])
        eastward = spar[which * 5 + 3] > 0.0
        for j, fe, fw in pairs:
            for row, ve, vw in ((j, fe, fw), (j + half, pltpu.roll(fe, LANES - EDGE, axis=1), pltpu.roll(fw, EDGE, axis=1))):
                o = own[which * LAT + row]
                xe = jnp.where(first, ve, o)
                xw = jnp.where(first, o, vw)
                s[row] = jnp.where(eastward, xe, xw)
                sm[row] = jnp.where(eastward, fan(xe, last), fan(xw, last))

    def write_strip(j, v):
        s[j] = v

    def strips_of(which):
        scoefs = [spar[which * 5 + k] for k in range(5)]

        @pl.loop(0, SUBSTEPS)
        def _(_k):
            sweep(lambda j: s[j], write_strip, lambda j: sm[j],
                  (scoefs[0], scoefs[1], scoefs[2], scoefs[3] > 0.0, scoefs[4] > 0.0))

    @pl.loop(0, EARLY)
    def _(g):
        main(g)

    to_east(0).wait_recv()
    to_west(0).wait_recv()

    @pl.loop(0, fourth // 4)
    def _(t):
        pairs = []
        for i in range(4):
            j = t * 4 + i
            fe, fw = ter[j], twr[j]
            pairs.append((j, fe, fw))
            pairs.append((j + fourth, pltpu.roll(fe, LANES - fold, axis=1), pltpu.roll(fw, LANES - fold, axis=1)))
        unpack(0, pairs)

    strips_of(0)

    @pl.loop(0, EARLY)
    def _(g):
        merge(g, 0)
        shuffle(g, 1)

    @pl.loop(EARLY, EARLY + 1)
    def _(g):
        main(g)

    for c in (1, 2):
        to_east(c).wait_recv()
        to_west(c).wait_recv()

        @pl.loop(0, half // 16)
        def _(t):
            rows = [(c - 1) * (half // 2) + t * 8 + i for i in range(8)]
            unpack(1, [(j, ter[fourth + j], twr[fourth + j]) for j in rows])

    strips_of(1)
    merge(EARLY, EARLY)

    @pl.loop(EARLY + 1, groups)
    def _(g):
        main(g)
        merge(g, EARLY)

    @pl.loop(EARLY, groups)
    def _(g):
        shuffle(g, 1)

    @pl.loop(0, total // (SUB * SUB))
    def _(t):
        tiles = [pl.ds(pl.multiple_of(t * SUB * SUB + i * SUB, SUB), SUB) for i in range(SUB)]
        kinds = [parts(kcol[at, :]) for at in tiles]
        for at, (direction, freq) in zip(tiles, kinds):
            for k, value in enumerate((look(1, freq), look(2, freq), look(4, direction), look(5, direction))):
                fpar[k, at, :] = value

    for g in range(groups):
        column = jnp.concatenate(
            [kcol[pl.ds(d * comps + g * SUB, SUB), :] for d in range(n)], axis=0)
        kq[:, g * LANES:(g + 1) * LANES] = column.T[:SUB]

    dirq, freqq = parts(kq[...])
    rowid = lax.broadcasted_iota(jnp.int32, (LANES, total), 0).astype(F32)
    colid = lax.broadcasted_iota(jnp.int32, (LANES, total), 1).astype(F32)

    def one_hot(hit):
        return hit.astype(F32).astype(BF16)

    share = shared * (1.0 / total)
    high = share.astype(BF16).astype(F32)
    both = jnp.concatenate([high, share - high], axis=0).astype(BF16)
    picked = jnp.dot(both, one_hot(jnp.broadcast_to(freqq[0:1], (LANES, total)) + 3.0 * FREQ == rowid), preferred_element_type=F32)
    w16[...] = jnp.concatenate([jnp.broadcast_to(picked[0:1], (SUB, total)),
                                jnp.broadcast_to(picked[SUB:SUB + 1], (SUB, total))], axis=0).astype(BF16)

    spx[...] = jnp.zeros_like(spx)
    spx[:, 0:DIRS] = sp[...]

    @pl.loop(0, total // LANES)
    def _(t):
        rows = pl.ds(pl.multiple_of(t * LANES, LANES), LANES)
        direction, freq = parts(kcol[rows, :])
        hot = one_hot(jnp.concatenate([direction * FREQ + freq] * (total // LANES), axis=1) == colid)
        same = jnp.concatenate([freq] * (total // LANES), axis=1) == jnp.broadcast_to(freqq[0:1], (LANES, total))
        pick = one_hot(jnp.broadcast_to(dirq[0:1], (LANES, total)) == rowid)
        full = spx[...]
        upper = full.astype(BF16)
        lower = (full - upper.astype(F32)).astype(BF16)
        for ref, table in ((cph, upper), (cpl, lower)):
            chosen = jnp.dot(hot, table, preferred_element_type=F32).astype(BF16)
            wide = jnp.dot(chosen, pick, preferred_element_type=F32)
            ref[rows, :] = jnp.where(same, wide, 0.0).astype(BF16)

    for j in range(block):
        ld[j] = jnp.zeros((SUB, LANES), F32)

        @pl.loop(0, total // LANES)
        def _(t):
            acc[j, pl.ds(pl.multiple_of(t * LANES, LANES), LANES), :] = jnp.zeros((LANES, LANES), F32)

    def split(jp, ks):
        e = jnp.concatenate([r[2 * jp, ks, :], r[2 * jp + 1, ks, :]], axis=1)
        hi = e.astype(BF16)
        return hi, (e - hi.astype(F32)).astype(BF16)

    def accumulate(jp, rows, ks, hi, lo):
        ch, cl = cph[rows, ks], cpl[rows, ks]
        part = (jnp.dot(ch, hi, preferred_element_type=F32) + jnp.dot(cl, hi, preferred_element_type=F32)
                + jnp.dot(ch, lo, preferred_element_type=F32))
        acc[2 * jp, rows, :] += part[:, :LANES]
        acc[2 * jp + 1, rows, :] += part[:, LANES:]

    def weigh(jp, ks, hi, lo):
        wh = jnp.dot(w16[:, ks], hi, preferred_element_type=F32)
        wl = jnp.dot(w16[:, ks], lo, preferred_element_type=F32)
        part = wh[:SUB] + wh[SUB:] + wl[:SUB]
        ld[2 * jp] += part[:, :LANES]
        ld[2 * jp + 1] += part[:, LANES:]

    chunk = total // 3

    tail = pl.ds((groups - 1) * span, span)
    quarter = n // 4
    base = lax.div(me, quarter)
    landed = lambda q, h: pl.ds(q * block + h * part, part)

    def sent(h, d):
        return outs.at[pl.ds((h * n + d) * part, part)]

    def back(h, d):
        k = h * n + lax.rem(d - me + n, n)
        return pltpu.make_async_remote_copy(
            src_ref=sent(h, d), dst_ref=land.at[landed(me, h)], send_sem=send2.at[k], recv_sem=recv2.at[k],
            device_id={"group": d}, device_id_type=MESH)

    def back_mine(h):
        return pltpu.make_async_copy(sent(h, me), land.at[landed(me, h)], recv2.at[h * n])

    def finish(h, d):
        @pl.loop(0, groups // 3)
        def _(t):
            for i in range(3):
                b = t * 3 + i
                at = pl.multiple_of(d * comps + b * SUB, SUB)
                grow, cap, cosine, sine = [fpar[k, pl.ds(at, SUB), :] for k in range(4)]
                for jr in range(part):
                    j = h * part + jr
                    e = r[j, pl.ds(pl.multiple_of(b * span + d * SUB, SUB), SUB), :]
                    u = jnp.broadcast_to(wind[pl.ds(j, 1), :], (SUB, LANES))
                    v = jnp.broadcast_to(wind[pl.ds(block + j, 1), :], (SUB, LANES))
                    power = grow * relu(cosine * u + sine * v) - cap * ld[j]
                    new = e * jnp.exp(power) + 0.5 * acc[j, pl.ds(at, SUB), :]
                    outs[(h * n + d) * part + jr, pl.ds(pl.multiple_of(b * SUB, SUB), SUB), :] = new * mb[me * block + j]

    def turn(c):
        return jnp.where(c == 0, 2, jnp.where(c == 1, 1, jnp.where(c == 2, 3, 0)))

    @pl.loop(0, HALVES)
    def _(h):
        pairs = part // 2

        @pl.loop(0, groups // 2)
        def _(b):
            arrive(2 * b, h)
            arrive(2 * b + 1, h)
            ks = pl.ds(pl.multiple_of(b * 2 * span, 2 * span), 2 * span)

            @pl.loop(0, pairs)
            def _(i):
                jp = h * pairs + i
                hi, lo = split(jp, ks)
                weigh(jp, ks, hi, lo)

                @pl.loop(0, 3)
                def _(m):
                    accumulate(jp, pl.ds(pl.multiple_of(m * chunk, chunk), chunk), ks, hi, lo)

        arrive(groups - 1, h)

        @pl.loop(0, pairs)
        def _(i):
            jp = h * pairs + i
            hi, lo = split(jp, tail)
            weigh(jp, tail, hi, lo)

        for jr in range(part):
            j = h * part + jr
            loading = ld[j]
            ld[j] = loading / (1.0 + loading)

        @pl.loop(0, 4)
        def _(c):
            m = lax.rem(base + turn(c), 4)
            rows = pl.ds(pl.multiple_of(m * quarter * comps, 16), quarter * comps)

            @pl.loop(0, pairs)
            def _(i):
                jp = h * pairs + i
                hi, lo = split(jp, tail)
                accumulate(jp, rows, tail, hi, lo)

            @pl.loop(0, quarter)
            def _(i):
                d = m * quarter + i
                finish(h, d)

                @pl.when(d != me)
                def _():
                    back(h, d).start()

                @pl.when(d == me)
                def _():
                    back_mine(h).start()

    @pl.loop(0, groups)
    def _(g):
        for h in range(HALVES):
            whole(g, h).wait_send()

    for c in range(PARTS):
        to_east(c).wait_send()
        to_west(c).wait_send()

    flat = stage.reshape(n * comps * block, LANES)

    def deliver(q):
        return pltpu.make_async_copy(
            stage.at[pl.ds(pl.multiple_of(q * comps, SUB), comps)],
            out.at[:, pl.ds(pl.multiple_of(q * block, block), block), :], done.at[q])

    def relayout(q):
        @pl.loop(0, groups // 3)
        def _(t):
            for i in range(3):
                b = t * 3 + i
                for j in range(block):
                    flat[pl.ds((q * comps + b * SUB) * block + j, SUB, stride=block), :] = (
                        land[q * block + j, pl.ds(pl.multiple_of(b * SUB, SUB), SUB), :])

        deliver(q).start()

    @pl.loop(0, 4)
    def _(c):
        m = lax.rem(base + 4 - turn(c), 4)

        @pl.when(c == 3)
        def _():
            @pl.loop(1, n)
            def _(k):
                for h in range(HALVES):
                    back(h, lax.rem(me + k, n)).wait_send()


        @pl.loop(0, quarter)
        def _(i):
            q = m * quarter + i
            k = lax.rem(me - q + n, n)

            @pl.when(q != me)
            def _():
                for h in range(HALVES):
                    back(h, lax.rem(me + k, n)).wait_recv()

            @pl.when(q == me)
            def _():
                for h in range(HALVES):
                    back_mine(h).wait()

            relayout(q)

    @pl.loop(0, n)
    def _(q):
        deliver(q).wait()


def local(n, ns, spectrum, land_mask, wind_field, assignment, courant, growth, whitecap, weights, spread):
    comps = spectrum.shape[0]
    total = assignment.shape[0]
    groups = comps // SUB
    block = LAT // n
    whole_small = jnp.concatenate((land_mask, jnp.pad(assignment.reshape(total // LANES, LANES), ((0, n - total // LANES), (0, 0)))))
    part_small = jnp.concatenate((wind_field.reshape(-1), courant, growth, whitecap, weights, jnp.zeros(((SUB - 1) * LANES,), F32)))
    part_small = part_small.reshape(3 * SUB, LANES)
    vmem = pl.BlockSpec(memory_space=pltpu.VMEM)
    tiles = lambda count: pltpu.VMEM((count, SUB, LANES), F32)
    dma = pltpu.SemaphoreType.DMA
    call = pl.pallas_call(
        functools.partial(kernel, n, ns, comps),
        out_shape=jax.ShapeDtypeStruct((comps, LAT, LANES), F32),
        in_specs=[pl.BlockSpec(memory_space=pl.ANY)] + [vmem] * 3,
        out_specs=pl.BlockSpec(memory_space=pl.ANY),
        scratch_shapes=[
            pltpu.VMEM((comps * LAT, LANES), F32),
            pltpu.VMEM((LAT, comps, LANES), F32),
            pltpu.VMEM((block, total, LANES), F32),
            pltpu.VMEM((block, total, LANES), F32),
            pltpu.VMEM((total, total), BF16),
            pltpu.VMEM((total, total), BF16),
            pltpu.VMEM((n * block, comps, LANES), F32),
            tiles(2 * LAT), tiles(LAT), tiles(LAT), tiles(LAT), tiles(LAT),
            tiles(LAT), tiles(LAT), tiles(LAT), tiles(block),
            pltpu.VMEM((2 * SUB, total), BF16),
            pltpu.SMEM((LAT,), F32),
            pltpu.VMEM((total, LANES), F32),
            pltpu.VMEM((SUB, total), F32),
            tiles(groups * 5), tiles(10),
            pltpu.VMEM((4, total, LANES), F32),
            pltpu.VMEM((total, LANES), F32),
            pltpu.VMEM((LAT, comps, LANES), F32),
            pltpu.VMEM((n * comps, block, LANES), F32),
            dma((groups,)), dma((2 * PARTS,)), dma((2 * PARTS,)),
            dma((groups * HALVES,)), dma((groups * HALVES,)), dma((groups * HALVES,)),
            dma((HALVES * n,)), dma((HALVES * n,)), dma((n,)),
        ],
        compiler_params=pltpu.CompilerParams(collective_id=0, has_side_effects=True, vmem_limit_bytes=48 << 20),
    )
    return call(spectrum.reshape(comps * LAT, LANES), whole_small, part_small, spread.transpose(1, 0, 2).reshape(FREQ * DIRS, DIRS))


def solution(mesh):
    in_specs = (P("group", None, "sector"), P(None, "sector"), P(None, "group", "sector"), P(), P(), P(), P(), P(), P())
    return jax.shard_map(functools.partial(local, mesh.shape["group"], mesh.shape["sector"]), mesh=mesh,
                         in_specs=in_specs, out_specs=P("group", None, "sector"), check_vma=False)
```

```python
import functools
import math

import jax
import jax.numpy as jnp
import numpy as np
from jax import lax
from jax.experimental import pallas as pl
from jax.experimental.pallas import tpu as pltpu
from jax.sharding import PartitionSpec as P

MESH = pl.DeviceIdType.MESH
DIRS = 36
FREQ = 32
SUBSTEPS = 6
LAT = 128
LANES = 128
EDGE = SUBSTEPS
SLOT = 2 * EDGE
SUB = 8
EARLY = 2
HALVES = 2
PARTS = 3
DEEP = 128
F32 = jnp.float32
BF16 = jnp.bfloat16


def relu(x):
    return jnp.maximum(x, 0.0)


def kernel(n, ns, comps, spec, whole_small, part_small, sp, out,
           x, p, r, acc, cph, cpl, outs, own, te, tw, ter, twr, s, sm, mb, ld, w16, icos,
           kcol, kq, cpar, spar, fpar, spx,
           land, stage,
           load_sem, halo_send, halo_recv, send1, recv1, mine1, send2, recv2, done):
    lm = whole_small.at[pl.ds(0, LAT)]
    asg = whole_small.at[pl.ds(LAT, n)]
    wind = part_small.at[pl.ds(0, 2 * SUB)]
    tabs = part_small.at[pl.ds(2 * SUB, SUB)]
    me = lax.axis_index("group")
    sec = lax.axis_index("sector")
    east, west = lax.rem(sec + 1, ns), lax.rem(sec + ns - 1, ns)
    total = n * comps
    groups = comps // SUB
    block = LAT // n
    span = n * SUB

    def load(g):
        rows = pl.ds(g * SUB * LAT, SUB * LAT)
        return pltpu.make_async_copy(spec.at[rows], x.at[rows], load_sem.at[g])

    for g in range(groups):
        load(g).start()

    barrier = pltpu.get_barrier_semaphore()

    @pl.loop(1, n)
    def _(k):
        pl.semaphore_signal(barrier, inc=1, device_id={"group": lax.rem(me + k, n)}, device_id_type=MESH)

    for side in (east, west):
        pl.semaphore_signal(barrier, inc=1, device_id={"sector": side}, device_id_type=MESH)

    lane = lax.broadcasted_iota(jnp.int32, (SUB, LANES), 1)
    first = lax.rem(lane, SLOT) < EDGE

    @pl.loop(0, LAT // SUB)
    def _(t):
        for i in range(SUB):
            j = t * SUB + i
            mb[j] = jnp.broadcast_to(lm[pl.ds(j, 1), :].astype(F32), (SUB, LANES))

    sets = [list(range(EARLY)), list(range(EARLY, groups))]
    for g in range(EARLY):
        load(g).wait()

    half = LAT // 2
    fourth = half // 2
    fold = SLOT * (EARLY + 1)

    def window(members, j):
        packed = pltpu.roll(mb[j], EDGE + SLOT * len(members), axis=1)
        for i, g in enumerate(members):
            tile = x[pl.ds(g * SUB * LAT + j, SUB, stride=LAT), :]
            tile = pltpu.roll(tile, EDGE + SLOT * i, axis=1)
            packed = jnp.where((lane >= SLOT * i) & (lane < SLOT * (i + 1)), tile, packed)
        return packed

    def pair(which, j):
        low, high = window(sets[which], j), window(sets[which], j + half)
        own[which * LAT + j] = low
        own[which * LAT + j + half] = high
        return (jnp.where(first, low, pltpu.roll(high, EDGE, axis=1)),
                jnp.where(first, pltpu.roll(high, LANES - EDGE, axis=1), low))

    def folded(a, b):
        return jnp.where(lane < fold, a, pltpu.roll(b, fold, axis=1))

    @pl.loop(0, fourth // 4)
    def _(t):
        for i in range(4):
            j = t * 4 + i
            ea, wa = pair(0, j)
            eb, wb = pair(0, j + fourth)
            te[j] = folded(ea, eb)
            tw[j] = folded(wa, wb)

    pl.semaphore_wait(barrier, n + 1)
    starts = [0, fourth, fourth + half // 2, fourth + half]

    def halo(src, dst, k, c, side):
        rows = pl.ds(starts[c], starts[c + 1] - starts[c])
        return pltpu.make_async_remote_copy(
            src_ref=src.at[rows], dst_ref=dst.at[rows], send_sem=halo_send.at[k * PARTS + c],
            recv_sem=halo_recv.at[k * PARTS + c], device_id={"sector": side}, device_id_type=MESH)

    def to_east(c):
        return halo(te, ter, 0, c, east)

    def to_west(c):
        return halo(tw, twr, 1, c, west)

    to_east(0).start()
    to_west(0).start()

    for g in range(EARLY, groups):
        load(g).wait()

    @pl.loop(0, half // 4)
    def _(t):
        for i in range(4):
            j = t * 4 + i
            te[fourth + j], tw[fourth + j] = pair(1, j)

    for c in (1, 2):
        to_east(c).start()
        to_west(c).start()

    for j in range(LAT):
        icos[j] = np.float32(1.0 / math.cos((j + 0.5 - LAT / 2) * (math.pi / 2160.0)))

    @pl.loop(0, total // LANES)
    def _(t):
        row = asg[pl.ds(t, 1), :].astype(F32)
        kcol[pl.ds(pl.multiple_of(t * LANES, LANES), LANES), :] = jnp.broadcast_to(row, (LANES, LANES)).T

    def parts(kind):
        freq = jnp.floor((kind + 0.5) * (1.0 / DIRS))
        return kind - DIRS * freq, freq

    lanef = lane.astype(F32)

    shared = jnp.broadcast_to(tabs[0:1, :], (SUB, LANES))
    tables = [shared] * 4
    for wave in (math.cos, math.sin):
        values = jnp.zeros((SUB, LANES), F32)
        for d in range(DIRS):
            values = jnp.where(lane == d, np.float32(wave((d + 0.5) * (2.0 * math.pi / DIRS))), values)
        tables.append(values)

    def look(k, index):
        hit = jnp.where(lanef == index + float(FREQ * k) if k < 4 else lanef == index, tables[k], 0.0)
        return jnp.broadcast_to(jnp.sum(hit, axis=1, keepdims=True), (SUB, LANES))

    strips = [[jnp.zeros((SUB, LANES), F32)] * 5 for _ in sets]
    for g in range(groups):
        which = 0 if g < EARLY else 1
        place = g - sets[which][0]
        direction, freq = parts(kcol[pl.ds(pl.multiple_of(me * comps + g * SUB, SUB), SUB), :])
        speed = look(0, freq)
        fx = speed * look(4, direction)
        fy = speed * look(5, direction)
        values = (jnp.abs(fx), 1.0 - jnp.abs(fy), jnp.abs(fy), (fx > 0.0).astype(F32), (fy > 0.0).astype(F32))
        slot = (lane >= SLOT * place) & (lane < SLOT * (place + 1))
        for k in range(5):
            cpar[g * 5 + k] = values[k]
            strips[which][k] = jnp.where(slot, values[k], strips[which][k])
    for which in range(2):
        for k in range(5):
            spar[which * 5 + k] = strips[which][k]

    def sweep(read, write, mask, coefs):
        rate, keep, north, sx, sy = coefs

        def rows(j0, prev, cur, nexts):
            tiles = [prev, cur] + nexts
            for i in range(DEEP):
                e = tiles[i + 1]
                fx = jnp.where(sx, pltpu.roll(e, 1, axis=1), pltpu.roll(e, LANES - 1, axis=1))
                fy = jnp.where(sy, tiles[i], tiles[i + 2])
                new = keep * e + north * fy + (rate * icos[j0 + i]) * (fx - e)
                write(j0 + i, new * mask(j0 + i))
            return tiles[DEEP], tiles[DEEP + 1]

        def body(t, carry):
            j0 = t * DEEP
            return rows(j0, *carry, [read(j0 + 1 + i) for i in range(DEEP)])

        zero = jnp.zeros((SUB, LANES), F32)
        prev, cur = lax.fori_loop(0, LAT // DEEP - 1, body, (zero, read(0)))
        j0 = LAT - DEEP
        rows(j0, prev, cur, [read(j0 + 1 + i) for i in range(DEEP - 1)] + [zero])

    def mask_row(j):
        return mb[j]

    def main(g):
        rate, keep, north, sx, sy = [cpar[g * 5 + k] for k in range(5)]
        coefs = (rate, keep, north, sx > 0.0, sy > 0.0)
        mine = pl.ds(pl.multiple_of(g * SUB, SUB), SUB)

        def write(j, v):
            p[j, mine, :] = v

        sweep(lambda j: x[pl.ds(g * SUB * LAT + j, SUB, stride=LAT), :], write, mask_row, coefs)

        @pl.loop(1, SUBSTEPS)
        def _(_k):
            sweep(lambda j: p[j, mine, :], write, mask_row, coefs)

    part = block // HALVES

    def source(g, h, peer):
        return p.at[pl.ds(peer * block + h * part, part), pl.ds(pl.multiple_of(g * SUB, SUB), SUB), :]

    def target(g, h):
        return r.at[pl.ds(h * part, part), pl.ds(pl.multiple_of(g * span + me * SUB, SUB), SUB), :]

    def shuffle(g, h):
        @pl.loop(1, n)
        def _(k):
            peer = lax.rem(me + k, n)
            pltpu.make_async_remote_copy(
                src_ref=source(g, h, peer), dst_ref=target(g, h), send_sem=send1.at[g * HALVES + h],
                recv_sem=recv1.at[g * HALVES + h], device_id={"group": peer}, device_id_type=MESH).start()

        keep_mine(g, h).start()

    def keep_mine(g, h):
        return pltpu.make_async_copy(source(g, h, me), target(g, h), mine1.at[g * HALVES + h])

    def whole(g, h):
        view = r.at[pl.ds(h * part, part), pl.ds(pl.multiple_of(g * span, SUB), span - SUB), :]
        return pltpu.make_async_remote_copy(
            src_ref=view, dst_ref=view, send_sem=send1.at[g * HALVES + h], recv_sem=recv1.at[g * HALVES + h],
            device_id={"group": lax.rem(me + 1, n)}, device_id_type=MESH)

    def arrive(g, h):
        whole(g, h).wait_recv()
        keep_mine(g, h).wait()

    def merge(g, origin):
        seam = jnp.where(cpar[g * 5 + 3] > 0.0, (lane < EDGE).astype(F32), (lane >= LANES - EDGE).astype(F32)) > 0.0
        mine = pl.ds(pl.multiple_of(g * SUB, SUB), SUB)
        shift = LANES - EDGE - SLOT * (g - origin)

        @pl.loop(0, LAT // (2 * SUB))
        def _(t):
            for i in range(2 * SUB):
                j = t * 2 * SUB + i
                p[j, mine, :] = jnp.where(seam, pltpu.roll(s[j], shift, axis=1), p[j, mine, :])

        shuffle(g, 0)

    def fan(v, last):
        v1 = jnp.where((lane >= SLOT * last) & (lane < SLOT * (last + 1)), v, 0.0)
        v2 = v1 + pltpu.roll(v1, LANES - SLOT, axis=1)
        v4 = v2 + pltpu.roll(v2, LANES - 2 * SLOT, axis=1)
        return v4 if last < 4 else v4 + pltpu.roll(v4, LANES - 4 * SLOT, axis=1)

    def unpack(which, pairs):
        last = len(sets[which])
        eastward = spar[which * 5 + 3] > 0.0
        for j, fe, fw in pairs:
            for row, ve, vw in ((j, fe, fw), (j + half, pltpu.roll(fe, LANES - EDGE, axis=1), pltpu.roll(fw, EDGE, axis=1))):
                o = own[which * LAT + row]
                xe = jnp.where(first, ve, o)
                xw = jnp.where(first, o, vw)
                s[row] = jnp.where(eastward, xe, xw)
                sm[row] = jnp.where(eastward, fan(xe, last), fan(xw, last))

    def write_strip(j, v):
        s[j] = v

    def strips_of(which):
        scoefs = [spar[which * 5 + k] for k in range(5)]

        @pl.loop(0, SUBSTEPS)
        def _(_k):
            sweep(lambda j: s[j], write_strip, lambda j: sm[j],
                  (scoefs[0], scoefs[1], scoefs[2], scoefs[3] > 0.0, scoefs[4] > 0.0))

    @pl.loop(0, EARLY)
    def _(g):
        main(g)

    to_east(0).wait_recv()
    to_west(0).wait_recv()

    @pl.loop(0, fourth // 4)
    def _(t):
        pairs = []
        for i in range(4):
            j = t * 4 + i
            fe, fw = ter[j], twr[j]
            pairs.append((j, fe, fw))
            pairs.append((j + fourth, pltpu.roll(fe, LANES - fold, axis=1), pltpu.roll(fw, LANES - fold, axis=1)))
        unpack(0, pairs)

    strips_of(0)

    @pl.loop(0, EARLY)
    def _(g):
        merge(g, 0)
        shuffle(g, 1)

    @pl.loop(EARLY, EARLY + 1)
    def _(g):
        main(g)

    for c in (1, 2):
        to_east(c).wait_recv()
        to_west(c).wait_recv()

        @pl.loop(0, half // 16)
        def _(t):
            rows = [(c - 1) * (half // 2) + t * 8 + i for i in range(8)]
            unpack(1, [(j, ter[fourth + j], twr[fourth + j]) for j in rows])

    strips_of(1)
    merge(EARLY, EARLY)

    @pl.loop(EARLY + 1, groups)
    def _(g):
        main(g)
        merge(g, EARLY)

    @pl.loop(EARLY, groups)
    def _(g):
        shuffle(g, 1)

    @pl.loop(0, total // (SUB * SUB))
    def _(t):
        tiles = [pl.ds(pl.multiple_of(t * SUB * SUB + i * SUB, SUB), SUB) for i in range(SUB)]
        kinds = [parts(kcol[at, :]) for at in tiles]
        for at, (direction, freq) in zip(tiles, kinds):
            for k, value in enumerate((look(1, freq), look(2, freq), look(4, direction), look(5, direction))):
                fpar[k, at, :] = value

    for g in range(groups):
        column = jnp.concatenate(
            [kcol[pl.ds(d * comps + g * SUB, SUB), :] for d in range(n)], axis=0)
        kq[:, g * LANES:(g + 1) * LANES] = column.T[:SUB]

    dirq, freqq = parts(kq[...])
    rowid = lax.broadcasted_iota(jnp.int32, (LANES, total), 0).astype(F32)
    colid = lax.broadcasted_iota(jnp.int32, (LANES, total), 1).astype(F32)

    def one_hot(hit):
        return hit.astype(F32).astype(BF16)

    share = shared * (1.0 / total)
    high = share.astype(BF16).astype(F32)
    both = jnp.concatenate([high, share - high], axis=0).astype(BF16)
    picked = jnp.dot(both, one_hot(jnp.broadcast_to(freqq[0:1], (LANES, total)) + 3.0 * FREQ == rowid), preferred_element_type=F32)
    w16[...] = jnp.concatenate([jnp.broadcast_to(picked[0:1], (SUB, total)),
                                jnp.broadcast_to(picked[SUB:SUB + 1], (SUB, total))], axis=0).astype(BF16)

    spx[...] = jnp.zeros_like(spx)
    spx[:, 0:DIRS] = sp[...]

    @pl.loop(0, total // LANES)
    def _(t):
        rows = pl.ds(pl.multiple_of(t * LANES, LANES), LANES)
        direction, freq = parts(kcol[rows, :])
        hot = one_hot(jnp.concatenate([direction * FREQ + freq] * (total // LANES), axis=1) == colid)
        same = jnp.concatenate([freq] * (total // LANES), axis=1) == jnp.broadcast_to(freqq[0:1], (LANES, total))
        pick = one_hot(jnp.broadcast_to(dirq[0:1], (LANES, total)) == rowid)
        full = spx[...]
        upper = full.astype(BF16)
        lower = (full - upper.astype(F32)).astype(BF16)
        for ref, table in ((cph, upper), (cpl, lower)):
            chosen = jnp.dot(hot, table, preferred_element_type=F32).astype(BF16)
            wide = jnp.dot(chosen, pick, preferred_element_type=F32)
            ref[rows, :] = jnp.where(same, wide, 0.0).astype(BF16)

    for j in range(block):
        ld[j] = jnp.zeros((SUB, LANES), F32)

        @pl.loop(0, total // LANES)
        def _(t):
            acc[j, pl.ds(pl.multiple_of(t * LANES, LANES), LANES), :] = jnp.zeros((LANES, LANES), F32)

    def split(jp, ks):
        e = jnp.concatenate([r[2 * jp, ks, :], r[2 * jp + 1, ks, :]], axis=1)
        hi = e.astype(BF16)
        return hi, (e - hi.astype(F32)).astype(BF16)

    def accumulate(jp, rows, ks, hi, lo):
        ch, cl = cph[rows, ks], cpl[rows, ks]
        part = (jnp.dot(ch, hi, preferred_element_type=F32) + jnp.dot(cl, hi, preferred_element_type=F32)
                + jnp.dot(ch, lo, preferred_element_type=F32))
        acc[2 * jp, rows, :] += part[:, :LANES]
        acc[2 * jp + 1, rows, :] += part[:, LANES:]

    def weigh(jp, ks, hi, lo):
        wh = jnp.dot(w16[:, ks], hi, preferred_element_type=F32)
        wl = jnp.dot(w16[:, ks], lo, preferred_element_type=F32)
        part = wh[:SUB] + wh[SUB:] + wl[:SUB]
        ld[2 * jp] += part[:, :LANES]
        ld[2 * jp + 1] += part[:, LANES:]

    chunk = total // 3

    tail = pl.ds((groups - 1) * span, span)
    quarter = n // 4
    base = lax.div(me, quarter)
    landed = lambda q, h: pl.ds(q * block + h * part, part)

    def sent(h, d):
        return outs.at[pl.ds((h * n + d) * part, part)]

    def back(h, d):
        k = h * n + lax.rem(d - me + n, n)
        return pltpu.make_async_remote_copy(
            src_ref=sent(h, d), dst_ref=land.at[landed(me, h)], send_sem=send2.at[k], recv_sem=recv2.at[k],
            device_id={"group": d}, device_id_type=MESH)

    def back_mine(h):
        return pltpu.make_async_copy(sent(h, me), land.at[landed(me, h)], recv2.at[h * n])

    def finish(h, d):
        @pl.loop(0, groups // 3)
        def _(t):
            for i in range(3):
                b = t * 3 + i
                at = pl.multiple_of(d * comps + b * SUB, SUB)
                grow, cap, cosine, sine = [fpar[k, pl.ds(at, SUB), :] for k in range(4)]
                for jr in range(part):
                    j = h * part + jr
                    e = r[j, pl.ds(pl.multiple_of(b * span + d * SUB, SUB), SUB), :]
                    u = jnp.broadcast_to(wind[pl.ds(j, 1), :], (SUB, LANES))
                    v = jnp.broadcast_to(wind[pl.ds(block + j, 1), :], (SUB, LANES))
                    power = grow * relu(cosine * u + sine * v) - cap * ld[j]
                    new = e * jnp.exp(power) + 0.5 * acc[j, pl.ds(at, SUB), :]
                    outs[(h * n + d) * part + jr, pl.ds(pl.multiple_of(b * SUB, SUB), SUB), :] = new * mb[me * block + j]

    def turn(c):
        return jnp.where(c == 0, 2, jnp.where(c == 1, 1, jnp.where(c == 2, 3, 0)))

    @pl.loop(0, HALVES)
    def _(h):
        pairs = part // 2

        @pl.loop(0, groups // 2)
        def _(b):
            arrive(2 * b, h)
            arrive(2 * b + 1, h)
            ks = pl.ds(pl.multiple_of(b * 2 * span, 2 * span), 2 * span)

            @pl.loop(0, pairs)
            def _(i):
                jp = h * pairs + i
                hi, lo = split(jp, ks)
                weigh(jp, ks, hi, lo)

                @pl.loop(0, 3)
                def _(m):
                    accumulate(jp, pl.ds(pl.multiple_of(m * chunk, chunk), chunk), ks, hi, lo)

        arrive(groups - 1, h)

        @pl.loop(0, pairs)
        def _(i):
            jp = h * pairs + i
            hi, lo = split(jp, tail)
            weigh(jp, tail, hi, lo)

        for jr in range(part):
            j = h * part + jr
            loading = ld[j]
            ld[j] = loading / (1.0 + loading)

        @pl.loop(0, 4)
        def _(c):
            m = lax.rem(base + turn(c), 4)
            rows = pl.ds(pl.multiple_of(m * quarter * comps, 16), quarter * comps)

            @pl.loop(0, pairs)
            def _(i):
                jp = h * pairs + i
                hi, lo = split(jp, tail)
                accumulate(jp, rows, tail, hi, lo)

            @pl.loop(0, quarter)
            def _(i):
                d = m * quarter + i
                finish(h, d)

                @pl.when(d != me)
                def _():
                    back(h, d).start()

                @pl.when(d == me)
                def _():
                    back_mine(h).start()

    @pl.loop(0, groups)
    def _(g):
        for h in range(HALVES):
            whole(g, h).wait_send()

    for c in range(PARTS):
        to_east(c).wait_send()
        to_west(c).wait_send()

    flat = stage.reshape(n * comps * block, LANES)

    def deliver(q):
        return pltpu.make_async_copy(
            stage.at[pl.ds(pl.multiple_of(q * comps, SUB), comps)],
            out.at[:, pl.ds(pl.multiple_of(q * block, block), block), :], done.at[q])

    def relayout(q):
        @pl.loop(0, groups // 3)
        def _(t):
            for i in range(3):
                b = t * 3 + i
                for j in range(block):
                    flat[pl.ds((q * comps + b * SUB) * block + j, SUB, stride=block), :] = (
                        land[q * block + j, pl.ds(pl.multiple_of(b * SUB, SUB), SUB), :])

        deliver(q).start()

    @pl.loop(0, 4)
    def _(c):
        m = lax.rem(base + 4 - turn(c), 4)

        @pl.when(c == 3)
        def _():
            @pl.loop(1, n)
            def _(k):
                for h in range(HALVES):
                    back(h, lax.rem(me + k, n)).wait_send()


        @pl.loop(0, quarter)
        def _(i):
            q = m * quarter + i
            k = lax.rem(me - q + n, n)

            @pl.when(q != me)
            def _():
                for h in range(HALVES):
                    back(h, lax.rem(me + k, n)).wait_recv()

            @pl.when(q == me)
            def _():
                for h in range(HALVES):
                    back_mine(h).wait()

            relayout(q)

    @pl.loop(0, n)
    def _(q):
        deliver(q).wait()


def local(n, ns, spectrum, land_mask, wind_field, assignment, courant, growth, whitecap, weights, spread):
    comps = spectrum.shape[0]
    total = assignment.shape[0]
    groups = comps // SUB
    block = LAT // n
    whole_small = jnp.concatenate((land_mask, jnp.pad(assignment.reshape(total // LANES, LANES), ((0, n - total // LANES), (0, 0)))))
    part_small = jnp.concatenate((wind_field.reshape(-1), courant, growth, whitecap, weights, jnp.zeros(((SUB - 1) * LANES,), F32)))
    part_small = part_small.reshape(3 * SUB, LANES)
    vmem = pl.BlockSpec(memory_space=pltpu.VMEM)
    tiles = lambda count: pltpu.VMEM((count, SUB, LANES), F32)
    dma = pltpu.SemaphoreType.DMA
    call = pl.pallas_call(
        functools.partial(kernel, n, ns, comps),
        out_shape=jax.ShapeDtypeStruct((comps, LAT, LANES), F32),
        in_specs=[pl.BlockSpec(memory_space=pl.ANY)] + [vmem] * 3,
        out_specs=pl.BlockSpec(memory_space=pl.ANY),
        scratch_shapes=[
            pltpu.VMEM((comps * LAT, LANES), F32),
            pltpu.VMEM((LAT, comps, LANES), F32),
            pltpu.VMEM((block, total, LANES), F32),
            pltpu.VMEM((block, total, LANES), F32),
            pltpu.VMEM((total, total), BF16),
            pltpu.VMEM((total, total), BF16),
            pltpu.VMEM((n * block, comps, LANES), F32),
            tiles(2 * LAT), tiles(LAT), tiles(LAT), tiles(LAT), tiles(LAT),
            tiles(LAT), tiles(LAT), tiles(LAT), tiles(block),
            pltpu.VMEM((2 * SUB, total), BF16),
            pltpu.SMEM((LAT,), F32),
            pltpu.VMEM((total, LANES), F32),
            pltpu.VMEM((SUB, total), F32),
            tiles(groups * 5), tiles(10),
            pltpu.VMEM((4, total, LANES), F32),
            pltpu.VMEM((total, LANES), F32),
            pltpu.VMEM((LAT, comps, LANES), F32),
            pltpu.VMEM((n * comps, block, LANES), F32),
            dma((groups,)), dma((2 * PARTS,)), dma((2 * PARTS,)),
            dma((groups * HALVES,)), dma((groups * HALVES,)), dma((groups * HALVES,)),
            dma((HALVES * n,)), dma((HALVES * n,)), dma((n,)),
        ],
        compiler_params=pltpu.CompilerParams(collective_id=0, has_side_effects=True, vmem_limit_bytes=48 << 20),
    )
    return call(spectrum.reshape(comps * LAT, LANES), whole_small, part_small, spread.transpose(1, 0, 2).reshape(FREQ * DIRS, DIRS))


def solution(mesh):
    in_specs = (P("group", None, "sector"), P(None, "sector"), P(None, "group", "sector"), P(), P(), P(), P(), P(), P())
    return jax.shard_map(functools.partial(local, mesh.shape["group"], mesh.shape["sector"]), mesh=mesh,
                         in_specs=in_specs, out_specs=P("group", None, "sector"), check_vma=False)
```
